512 devices in a mesh: phi: 8 (over z), theta: 16 (over y, core), row: 4 (over x).
Axes of the slice: x: 4, y: 8, z: 8, core: 2. Of those that a mesh axis runs over, the one named last changes fastest.
Arguments:
- fields: float32 [8, 12, 1536, 2048], P(None, 'row', 'phi', 'theta'), may hold values from -6 to 6
- kept_counts: int32 [512], replicated, may hold values from 1 to 384, as said below
Outputs:
- filtered: float32 [8, 12, 1536, 2048], P(None, 'row', 'phi', 'theta')
The draws below stay inside these ranges and needn't reach their ends.
Inputs may be any that keep to these rules, and one draw needn't show every extreme that they name: `kept_counts`: modes 0 to count - 1 of a cap row are kept; some row reaches 384 in every draw.
All inputs are finite; a program needn't handle non-finite values.
Results may differ from the reference program's by a relative error of at most 0.00007.
Values sent between devices are 32-bit elements; how exact they have to be, the bound alone decides.
No kernel may reach another device: no remote copies, remote signals or barrier semaphores. Data moves between devices by JAX's collectives and lax.ppermute only.
A program may use at most 64 MiB of HBM per device.

```python
import jax
import jax.numpy as jnp
from jax import lax

NPHI = 1536
KMAX = 384
FIELDS = 8
CAP_BANDS = 2
TH_DEV = 128
NTH = 2048
NR = 12


def draw_kept_counts(key, part):
    cap_total = 2 * CAP_BANDS * TH_DEV
    values = jax.random.randint(jax.random.fold_in(key, 11), (cap_total,), 1, KMAX + 1)
    position = jax.random.randint(jax.random.fold_in(key, 12), (), 0, cap_total)
    return values.at[position].set(KMAX).astype(jnp.int32)


def levels(own_key, dims, cuts, low, high):
    level = 1.0
    for dim, blocks in cuts:
        steps = jax.random.uniform(jax.random.fold_in(jax.random.fold_in(own_key, 6), dim), (blocks,), jnp.float32, low / len(cuts), high / len(cuts))
        level = level * jnp.repeat(jnp.exp(steps), dims[dim] // blocks).reshape((-1,) + (1,) * (len(dims) - 1 - dim))
    return level


def gaussian(key, shape, deviation, bound, cuts=(), held_as=jnp.bfloat16):
    result = deviation * jax.random.normal(key, shape, jnp.float32)
    if cuts:
        result = result * levels(key, shape, cuts, -0.22, 0.18)
    return jnp.clip(result, -bound, bound).astype(held_as)


def setup_inputs(seed: int = 0) -> dict:
    arg_keys = jax.random.split(jax.random.key(seed), 3)
    return {
        "fields": gaussian(arg_keys[0], (FIELDS, NR, NPHI, NTH), 1.0, 6.0, ((1, 4), (2, 8), (3, 16)), jnp.float32),
        "kept_counts": draw_kept_counts(jax.random.fold_in(arg_keys[2], 71), 0),
    }


def reference(fields, kept_counts):
    cap_rows = CAP_BANDS * TH_DEV
    north = fields[:, :, :, :cap_rows]
    south = fields[:, :, :, NTH - cap_rows:]
    caps = jnp.concatenate([north, south], axis=3)
    wavenumber = jnp.arange(NPHI // 2 + 1, dtype=jnp.int32)
    keep = wavenumber[:, None] < kept_counts[None, :]

    def filter_field(field):
        spectrum = jnp.fft.rfft(field, axis=1)
        spectrum = jnp.where(keep[None, :, :], spectrum, 0.0)
        return jnp.fft.irfft(spectrum, n=NPHI, axis=1).astype(jnp.float32)

    smoothed = lax.map(filter_field, caps)
    middle = fields[:, :, :, cap_rows:NTH - cap_rows]
    return jnp.concatenate([smoothed[:, :, :, :cap_rows], middle, smoothed[:, :, :, cap_rows:]], axis=3)
```

```python
import math

import jax
import jax.numpy as jnp
import numpy as np
from jax import lax
from jax.experimental import pallas as pl
from jax.experimental.pallas import tpu as pltpu
from jax.sharding import PartitionSpec as P

KMAX = 384
NPHI = 1536
SEG = 8
LOC = NPHI // SEG
MODES = KMAX // SEG


def class_modes():
    m = SEG * np.arange(MODES)
    return [m, m + 4], [(m + p, m + SEG - p) for p in (1, 2, 3)]


def cos_sin(k):
    turns = (k[:, None] * np.arange(LOC)[None, :]) % NPHI
    angle = turns * (2.0 * math.pi / NPHI)
    return np.cos(angle), np.sin(angle)


def split(table):
    high = table.astype(jnp.bfloat16)
    low = (table - high.astype(np.float64)).astype(jnp.bfloat16)
    return high, low


def tables():
    real, paired = class_modes()
    mr = np.stack([np.concatenate(cos_sin(k)) for k in real])
    rows = []
    for kp, kn in paired:
        cp, sp = cos_sin(kp)
        cn, sn = cos_sin(kn)
        rows.append(
            np.concatenate(
                [
                    np.concatenate([cp, -sp], 1),
                    np.concatenate([cn, sn], 1),
                    np.concatenate([sp, cp], 1),
                    np.concatenate([sn, -cn], 1),
                ]
            )
        )
    mp = np.stack(rows)
    kr = np.stack([np.concatenate([k, k]) for k in real])
    kp = np.stack([np.concatenate([a, b, a, b]) for a, b in paired])
    modes = np.concatenate([kr.reshape(-1), kp.reshape(-1)]).astype(np.int32)
    return mr, mp, modes


def dot(a, b):
    return lax.dot_general(a, b, (((1,), (0,)), ((), ())), preferred_element_type=jnp.float32)


def dot3(high, low, x):
    xh = x.astype(jnp.bfloat16)
    xl = (x - xh.astype(jnp.float32)).astype(jnp.bfloat16)
    return dot(high, xh) + (dot(high, xl) + dot(low, xh))


HALF = math.sqrt(0.5)


def filter_body(y_ref, counts_ref, modes_ref, arh, arl, aph, apl, brh, brl, bph, bpl, o_ref):
    counts = counts_ref[...]
    f = [y_ref[s] for s in range(SEG)]
    e = [f[i] + f[i + 4] for i in range(4)]
    o = [f[i] - f[i + 4] for i in range(4)]
    e02, e13 = e[0] + e[2], e[1] + e[3]
    od, os_ = HALF * (o[1] - o[3]), HALF * (o[1] + o[3])
    real = [e02 + e13, e02 - e13]
    pair = [
        (o[0] + od, o[2] + os_),
        (e[0] - e[2], e[1] - e[3]),
        (o[0] - od, os_ - o[2]),
    ]

    def keep(coef, at):
        k = modes_ref[at : at + coef.shape[0], :]
        weight = jnp.where(k == 0, 1.0 / NPHI, 2.0 / NPHI)
        return jnp.where(k < counts, coef * weight, 0.0)

    u = []
    for i in range(2):
        coef = keep(dot3(arh[i], arl[i], real[i]), i * 2 * MODES)
        u.append(dot3(brh[i], brl[i], coef))
    uv = []
    for i in range(3):
        x = jnp.concatenate(pair[i], axis=0)
        coef = keep(dot3(aph[i], apl[i], x), 4 * MODES + i * 4 * MODES)
        r = dot3(bph[i], bpl[i], coef)
        uv.append((r[:LOC], r[LOC:]))
    (u1, v1), (u2, v2), (u3, v3) = uv
    su, du = u[0] + u[1], u[0] - u[1]
    p = [su + u2, du + v2, su - u2, du - v2]
    d13, s13 = HALF * (u1 - u3), HALF * (v1 + v3)
    q = [u1 + u3, s13 + d13, v1 - v3, s13 - d13]
    for s in range(4):
        o_ref[s] = p[s] + q[s]
        o_ref[s + 4] = p[s] - q[s]


def solution(mesh):
    n_theta = mesh.shape["theta"]
    mr, mp, modes = tables()
    consts = (
        *split(mr),
        *split(mp),
        *split(np.swapaxes(mr, 1, 2)),
        *split(np.swapaxes(mp, 1, 2)),
    )
    modes = np.ascontiguousarray(np.broadcast_to(modes[:, None], (modes.size, 128)))
    last = n_theta - 1
    outward = [(0, 2), (1, 3), (last - 1, last - 3), (last, last - 2)]
    inward = [(b, a) for a, b in outward]

    def exchange(v):
        return lax.all_to_all(v, "phi", split_axis=0, concat_axis=0, tiled=True)

    def filter_lines(lines, counts):
        return pl.pallas_call(
            filter_body,
            out_shape=jax.ShapeDtypeStruct(lines.shape, jnp.float32),
            name="filter_lines",
        )(lines, counts, jnp.asarray(modes), *[jnp.asarray(c) for c in consts])

    def on_device(fields, kept_counts):
        theta = lax.axis_index("theta")
        is_cap = (theta < 2) | (theta > last - 2)
        is_helper = ((theta >= 2) & (theta < 4)) | ((theta > last - 4) & (theta <= last - 2))
        band = theta % 2 + jnp.where(theta < n_theta // 2, 0, 2)
        rows = fields.shape[3]
        counts = lax.dynamic_slice(kept_counts, (band * rows,), (rows,)).reshape(1, rows)
        x0, x1, x2 = fields[:, 0], fields[:, 1], fields[:, 2]
        moved = lax.ppermute(x2, "theta", outward)
        lines0 = exchange(x0)
        lines1 = exchange(jnp.where(is_helper, moved, x1))
        done0 = filter_lines(lines0, counts)
        done1 = filter_lines(lines1, counts)
        back0 = exchange(jnp.where(is_helper, done1, done0))
        back1 = exchange(done1)
        back2 = lax.ppermute(back0, "theta", inward)
        out = jnp.stack([back0, back1, back2], axis=1)
        return jnp.where(is_cap, out, fields)

    return jax.shard_map(
        on_device,
        mesh=mesh,
        in_specs=(P(None, "row", "phi", "theta"), P()),
        out_specs=P(None, "row", "phi", "theta"),
        check_vma=False,
    )
```

```python
import math

import jax
import jax.numpy as jnp
import numpy as np
from jax import lax
from jax.experimental import pallas as pl
from jax.experimental.pallas import tpu as pltpu
from jax.sharding import PartitionSpec as P

KMAX = 384
NPHI = 1536
SEG = 8
LOC = NPHI // SEG
MODES = KMAX // SEG


def class_modes():
    m = SEG * np.arange(MODES)
    return [m, m + 4], [(m + p, m + SEG - p) for p in (1, 2, 3)]


def cos_sin(k):
    turns = (k[:, None] * np.arange(LOC)[None, :]) % NPHI
    angle = turns * (2.0 * math.pi / NPHI)
    return np.cos(angle), np.sin(angle)


def split(table):
    high = table.astype(jnp.bfloat16)
    low = (table - high.astype(np.float64)).astype(jnp.bfloat16)
    return np.concatenate([high, low], axis=-2)


def tables():
    real, paired = class_modes()
    mr = np.stack([np.concatenate(cos_sin(k)) for k in real])
    rows = []
    for kp, kn in paired:
        cp, sp = cos_sin(kp)
        cn, sn = cos_sin(kn)
        rows.append(
            np.concatenate(
                [
                    np.concatenate([cp, -sp], 1),
                    np.concatenate([cn, sn], 1),
                    np.concatenate([sp, cp], 1),
                    np.concatenate([sn, -cn], 1),
                ]
            )
        )
    mp = np.stack(rows)
    kr = np.stack([np.concatenate([k, k]) for k in real])
    kp = np.stack([np.concatenate([a, b, a, b]) for a, b in paired])
    modes = np.concatenate([kr.reshape(-1), kp.reshape(-1)]).astype(np.int32)
    return mr, mp, modes


def dot(parts, x):
    high = x.astype(jnp.bfloat16)
    low = (x - high.astype(jnp.float32)).astype(jnp.bfloat16)
    both = jnp.concatenate([high, low], axis=1)
    r = lax.dot_general(parts, both, (((1,), (0,)), ((), ())), preferred_element_type=jnp.float32)
    n, c = parts.shape[0] // 2, x.shape[1]
    return r[:n, :c] + (r[:n, c:] + r[n:, :c] + r[n:, c:])


HALF = math.sqrt(0.5)


def filter_lines(y, counts, modes, ar, ap, br, bp):
    e = [y[i] + y[i + 4] for i in range(4)]
    o = [y[i] - y[i + 4] for i in range(4)]
    e02, e13 = e[0] + e[2], e[1] + e[3]
    od, os_ = HALF * (o[1] - o[3]), HALF * (o[1] + o[3])
    real = [e02 + e13, e02 - e13]
    pair = [
        (o[0] + od, o[2] + os_),
        (e[0] - e[2], e[1] - e[3]),
        (o[0] - od, os_ - o[2]),
    ]

    def keep(coef, at):
        k = modes[at : at + coef.shape[0], :]
        weight = jnp.where(k == 0, 1.0 / NPHI, 2.0 / NPHI)
        return jnp.where(k < counts, coef * weight, 0.0)

    u = [dot(br[i], keep(dot(ar[i], real[i]), i * 2 * MODES)) for i in range(2)]
    uv = []
    for i in range(3):
        coef = dot(ap[i], jnp.concatenate(pair[i], axis=0))
        r = dot(bp[i], keep(coef, 4 * MODES + i * 4 * MODES))
        uv.append((r[:LOC], r[LOC:]))
    (u1, v1), (u2, v2), (u3, v3) = uv
    su, du = u[0] + u[1], u[0] - u[1]
    p = [su + u2, du + v2, su - u2, du - v2]
    d13, s13 = HALF * (u1 - u3), HALF * (v1 + v3)
    q = [u1 + u3, s13 + d13, v1 - v3, s13 - d13]
    return [p[i] + q[i] for i in range(4)] + [p[i] - q[i] for i in range(4)]


def filter_kernel(cap_ref, y_ref, counts_ref, modes_ref, ar, ap, br, bp, o_ref):
    is_cap = cap_ref[0] > 0
    shells = y_ref.shape[1]

    @pl.when(is_cap)
    def _():
        @pl.loop(0, shells)
        def _(i):
            y = [y_ref[s, i] for s in range(SEG)]
            done = filter_lines(y, counts_ref[...], modes_ref, ar, ap, br, bp)
            for s in range(SEG):
                o_ref[s, i] = done[s]

    @pl.when(jnp.logical_not(is_cap))
    def _():
        o_ref[...] = y_ref[...]


def solution(mesh):
    last = mesh.shape["theta"] - 1
    mr, mp, modes = tables()
    modes = np.ascontiguousarray(np.broadcast_to(modes[:, None], (modes.size, 128)))
    consts = (modes, split(mr), split(mp), split(np.swapaxes(mr, 1, 2)), split(np.swapaxes(mp, 1, 2)))

    def exchange(v):
        return lax.all_to_all(v, "phi", split_axis=0, concat_axis=0, tiled=True)

    def filtered(lines, counts, is_cap):
        vmem = pl.BlockSpec(memory_space=pltpu.VMEM)
        return pl.pallas_call(
            filter_kernel,
            out_shape=jax.ShapeDtypeStruct(lines.shape, jnp.float32),
            in_specs=[pl.BlockSpec(memory_space=pltpu.SMEM)] + [vmem] * 7,
            out_specs=vmem,
            compiler_params=pltpu.CompilerParams(vmem_limit_bytes=16 << 20),
            name="filter_lines",
        )(is_cap.astype(jnp.int32).reshape(1), lines, counts, *[jnp.asarray(c) for c in consts])

    def on_device(fields, kept_counts):
        theta = lax.axis_index("theta")
        is_cap = (theta < 2) | (theta > last - 2)
        band = jnp.where(theta < 2, theta, theta - (last - 3)) % 4
        rows = fields.shape[3]
        counts = lax.dynamic_slice(kept_counts, (band * rows,), (rows,)).reshape(1, rows)
        return exchange(filtered(exchange(fields), counts, is_cap))

    return jax.shard_map(
        on_device,
        mesh=mesh,
        in_specs=(P(None, "row", "phi", "theta"), P()),
        out_specs=P(None, "row", "phi", "theta"),
        check_vma=False,
    )
```

```python
import math

import jax
import jax.numpy as jnp
import numpy as np
from jax import lax
from jax.experimental import pallas as pl
from jax.experimental.pallas import tpu as pltpu
from jax.sharding import PartitionSpec as P

KMAX = 384
NPHI = 1536
SEG = 8
LOC = NPHI // SEG
MODES = KMAX // SEG
HALF = math.sqrt(0.5)


def cos_sin(k):
    turns = (k[:, None] * np.arange(LOC)[None, :]) % NPHI
    angle = turns * (2.0 * math.pi / NPHI)
    return np.cos(angle), np.sin(angle)


def matrices():
    m = SEG * np.arange(MODES)
    zero, four = (np.concatenate(cos_sin(k)) for k in (m, m + 4))
    out = [zero, four]
    back = [np.concatenate([zero, four]).T, np.concatenate([zero, -four]).T]
    for p in (1, 2, 3):
        cp, sp = cos_sin(m + p)
        cn, sn = cos_sin(m + SEG - p)
        on_cos = np.concatenate([cp, cn, sp, sn])
        on_sin = np.concatenate([-sp, sn, cp, -cn])
        out += [on_cos, on_sin]
        back.append(np.concatenate([on_cos.T, on_sin.T]))
    return out + back


def table():
    parts, places, at = [], [], 0
    for m in matrices():
        high = m.astype(jnp.bfloat16)
        parts += [high, (m - high.astype(np.float64)).astype(jnp.bfloat16)]
        places.append((at, 2 * m.shape[0]))
        at += 2 * m.shape[0]
    return np.concatenate(parts), places


TABLE, PLACES = table()


def halves(x):
    high = x.astype(jnp.bfloat16)
    low = (x - high.astype(jnp.float32)).astype(jnp.bfloat16)
    return jnp.concatenate([high, low], axis=1)


def quarters(r):
    n, c = r.shape[0] // 2, r.shape[1] // 2
    return r[:n, :c] + (r[:n, c:] + r[n:, :c] + r[n:, c:])


def class_modes(*offsets):
    m = SEG * lax.broadcasted_iota(jnp.int32, (MODES, 128), 0)
    return jnp.concatenate([m + p for p in offsets], axis=0)


def filter_lines(y, counts, table_ref):
    def dot(i, x):
        at, n = PLACES[i]
        rows = table_ref[at : at + n, :]
        return lax.dot_general(rows, x, (((1,), (0,)), ((), ())), preferred_element_type=jnp.float32)

    def keep(coef, k):
        weight = jnp.where(k == 0, 1.0 / NPHI, 2.0 / NPHI)
        return halves(jnp.where(k < counts, coef * weight, 0.0))

    e = [y[i] + y[i + 4] for i in range(4)]
    o = [y[i] - y[i + 4] for i in range(4)]
    e02, e13 = e[0] + e[2], e[1] + e[3]
    od, os_ = HALF * (o[1] - o[3]), HALF * (o[1] + o[3])
    pairs = [
        (o[0] + od, o[2] + os_),
        (e[0] - e[2], e[1] - e[3]),
        (o[0] - od, os_ - o[2]),
    ]
    zero, four = quarters(dot(0, halves(e02 + e13))), quarters(dot(1, halves(e02 - e13)))
    both = keep(jnp.concatenate([zero, four], axis=0), class_modes(0, 0, 4, 4))
    su, du = quarters(dot(8, both)), quarters(dot(9, both))
    uv = []
    for p in (1, 2, 3):
        c, s = pairs[p - 1]
        coef = quarters(dot(2 * p, halves(c)) + dot(2 * p + 1, halves(s)))
        r = quarters(dot(9 + p, keep(coef, class_modes(p, SEG - p, p, SEG - p))))
        uv.append((r[:LOC], r[LOC:]))
    (u1, v1), (u2, v2), (u3, v3) = uv
    p = [su + u2, du + v2, su - u2, du - v2]
    d13, s13 = HALF * (u1 - u3), HALF * (v1 + v3)
    q = [u1 + u3, s13 + d13, v1 - v3, s13 - d13]
    return [p[i] + q[i] for i in range(4)] + [p[i] - q[i] for i in range(4)]


def gather_kernel(role_ref, x_ref, kept_ref, *refs):
    sent, sem = refs[:SEG], refs[SEG]
    stay = kept_ref.shape[0]
    copies = [pltpu.make_async_copy(x_ref.at[pl.ds(0, stay)], kept_ref, sem.at[SEG])]
    for d in range(SEG):
        group = stay + lax.rem(role_ref[1] + d, SEG)
        copies.append(pltpu.make_async_copy(x_ref.at[group], sent[d], sem.at[d]))
    for c in copies:
        c.start()
    for c in copies:
        c.wait()


def table_kernel(table_ref, o_ref, sem):
    copy = pltpu.make_async_copy(table_ref, o_ref, sem)
    copy.start()
    copy.wait()


def filter_kernel(role_ref, lines_ref, *refs):
    got, (counts_ref, table_ref, even_ref, odd_ref, turned) = refs[:SEG], refs[SEG:]

    @pl.when(role_ref[0] == 1)
    def _():
        for i, o_ref in ((0, even_ref), (1, odd_ref)):
            done = filter_lines([lines_ref[s, i] for s in range(SEG)], counts_ref[...], table_ref)
            for s in range(SEG):
                o_ref[s] = done[s]

    @pl.when(role_ref[0] == 2)
    def _():
        for d in range(SEG):
            turned[lax.rem(role_ref[1] + SEG - d, SEG)] = got[d][...]
        done = filter_lines([turned[s] for s in range(SEG)], counts_ref[...], table_ref)
        for s in range(SEG):
            even_ref[s] = done[s]


def finish_kernel(role_ref, x_ref, even_ref, odd_ref, home_ref, o_ref, sem):
    stay = 2 * SEG

    def run(copies):
        for c in copies:
            c.start()
        for c in copies:
            c.wait()

    @pl.when(role_ref[0] == 1)
    def _():
        copies = [pltpu.make_async_copy(home_ref, o_ref.at[pl.ds(stay, SEG)], sem.at[stay])]
        for s in range(SEG):
            copies.append(pltpu.make_async_copy(even_ref.at[s], o_ref.at[2 * s], sem.at[2 * s]))
            copies.append(pltpu.make_async_copy(odd_ref.at[s], o_ref.at[2 * s + 1], sem.at[2 * s + 1]))
        run(copies)

    @pl.when(role_ref[0] != 1)
    def _():
        run([pltpu.make_async_copy(x_ref, o_ref, sem.at[0])])


def solution(mesh):
    n_phi, n_theta, n_row = (mesh.shape[a] for a in ("phi", "theta", "row"))
    last = n_theta - 1
    caps, helpers = (0, 1, last - 1, last), (2, 3, last - 3, last - 2)

    def at(z, t, r):
        return (z * n_theta + t) * n_row + r

    groups = [[at(z, t, r) for z in range(n_phi)] for t in caps for r in range(n_row)]
    for t in range(2, last - 1, 2):
        for z in range(n_phi):
            groups.append([at(z, t + c, r) for r in range(n_row) for c in range(2)])

    def outward(d):
        return [
            (z * n_theta + a, (z + d) % n_phi * n_theta + b)
            for z in range(n_phi)
            for a, b in zip(caps, helpers)
        ]

    smem, vmem, hbm, either = (
        pl.BlockSpec(memory_space=m) for m in (pltpu.SMEM, pltpu.VMEM, pltpu.HBM, pl.ANY)
    )
    small = pltpu.CompilerParams(vmem_limit_bytes=16 << 20)

    def exchange(v):
        return lax.all_to_all(v, "phi", split_axis=0, concat_axis=0, tiled=True)

    def on_device(fields, kept_counts):
        nf, shells, points, rows = fields.shape
        total = nf * shells
        stay = total - SEG
        theta, z = lax.axis_index("theta"), lax.axis_index("phi")
        is_cap = (theta < 2) | (theta > last - 2)
        is_helper = ((theta >= 2) & (theta < 4)) | ((theta > last - 4) & (theta <= last - 2))
        role = jnp.stack([jnp.where(is_cap, 1, jnp.where(is_helper, 2, 0)), z]).astype(jnp.int32)
        band = jnp.bitwise_and(theta, 1) + jnp.where(theta < n_theta // 2, 0, 2)
        counts = lax.dynamic_slice(kept_counts, (band * rows,), (rows,)).reshape(1, rows)
        x = fields.reshape(total, points, rows)
        one = jax.ShapeDtypeStruct((points, rows), jnp.float32)
        some = jax.ShapeDtypeStruct((SEG, points, rows), jnp.float32)
        kept, *sent = pl.pallas_call(
            gather_kernel,
            out_shape=[jax.ShapeDtypeStruct((stay, points, rows), jnp.float32)] + [one] * SEG,
            in_specs=[smem, hbm],
            out_specs=[either] + [vmem] * SEG,
            scratch_shapes=[pltpu.SemaphoreType.DMA((SEG + 1,))],
            compiler_params=small,
            name="gather_groups",
        )(role, x)
        lines = lax.all_to_all(
            kept,
            ("phi", "theta", "row"),
            split_axis=0,
            concat_axis=0,
            tiled=True,
            axis_index_groups=groups,
        )
        got = [lax.ppermute(sent[d], ("phi", "theta"), outward(d)) for d in range(SEG)]
        matrix = pl.pallas_call(
            table_kernel,
            out_shape=jax.ShapeDtypeStruct(TABLE.shape, TABLE.dtype),
            in_specs=[hbm],
            out_specs=vmem,
            scratch_shapes=[pltpu.SemaphoreType.DMA],
            compiler_params=small,
            name="load_table",
        )(jnp.asarray(TABLE))
        even, odd = pl.pallas_call(
            filter_kernel,
            out_shape=[some, some],
            in_specs=[smem] + [vmem] * (SEG + 3),
            out_specs=[vmem, vmem],
            scratch_shapes=[pltpu.VMEM((SEG, points, rows), jnp.float32)],
            compiler_params=small,
            name="filter_lines",
        )(role, lines.reshape(SEG, 2, points, rows), *got, counts, matrix)
        even = exchange(even)
        odd = exchange(odd)
        home = lax.ppermute(even, "theta", [(b, a) for a, b in zip(caps, helpers)])
        out = pl.pallas_call(
            finish_kernel,
            out_shape=jax.ShapeDtypeStruct(x.shape, x.dtype),
            in_specs=[smem, hbm, either, either, either],
            out_specs=hbm,
            scratch_shapes=[pltpu.SemaphoreType.DMA((2 * SEG + 1,))],
            compiler_params=small,
            name="finish",
        )(role, x, even, odd, home)
        return out.reshape(fields.shape)

    return jax.shard_map(
        on_device,
        mesh=mesh,
        in_specs=(P(None, "row", "phi", "theta"), P()),
        out_specs=P(None, "row", "phi", "theta"),
        check_vma=False,
    )
```

```python
import math

import jax
import jax.numpy as jnp
import numpy as np
from jax import lax
from jax.experimental import pallas as pl
from jax.experimental.pallas import tpu as pltpu
from jax.sharding import PartitionSpec as P

KMAX = 384
NPHI = 1536
SEG = 8
LOC = NPHI // SEG
MODES = KMAX // SEG
HALF = math.sqrt(0.5)


def cos_sin(k):
    turns = (k[:, None] * np.arange(LOC)[None, :]) % NPHI
    angle = turns * (2.0 * math.pi / NPHI)
    return np.cos(angle), np.sin(angle)


def matrices():
    m = SEG * np.arange(MODES)
    real = [np.concatenate(cos_sin(k)) for k in (m, m + 4)]
    paired = []
    for p in (1, 2, 3):
        cp, sp = cos_sin(m + p)
        cn, sn = cos_sin(m + SEG - p)
        paired.append(np.block([[cp, -sp], [cn, sn], [sp, cp], [sn, -cn]]))
    return paired, real + [a.T for a in paired], [a.T for a in real]


def stacked(group):
    parts = []
    for m in group:
        high = m.astype(jnp.bfloat16)
        parts += [high, (m - high.astype(np.float64)).astype(jnp.bfloat16)]
    return np.concatenate(parts)


TABLES = [stacked(g) for g in matrices()]
PLACES = [[2 * sum(m.shape[0] for m in g[:i]) for i in range(len(g) + 1)] for g in matrices()]
STAY = 2 * SEG
FAR = (4, 3, 5, 2, 6)
NEAR = (0, 1, 7)


def halves(x):
    high = x.astype(jnp.bfloat16)
    low = (x - high.astype(jnp.float32)).astype(jnp.bfloat16)
    return jnp.concatenate([high, low], axis=1)


def quarters(r):
    n, c = r.shape[0] // 2, r.shape[1] // 2
    return r[:n, :c] + (r[:n, c:] + r[n:, :c] + r[n:, c:])


def class_modes(*offsets):
    m = SEG * lax.broadcasted_iota(jnp.int32, (MODES, 128), 0)
    return jnp.concatenate([m + p for p in offsets], axis=0)


def filter_lines(y, counts, tables):
    def dot(g, i, x):
        rows = tables[g][PLACES[g][i] : PLACES[g][i + 1], :]
        return quarters(lax.dot_general(rows, x, (((1,), (0,)), ((), ())), preferred_element_type=jnp.float32))

    def keep(coef, k):
        weight = jnp.where(k == 0, 1.0 / NPHI, 2.0 / NPHI)
        return halves(jnp.where(k < counts, coef * weight, 0.0))

    e = [y[i] + y[i + 4] for i in range(4)]
    o = [y[i] - y[i + 4] for i in range(4)]
    e02, e13 = e[0] + e[2], e[1] + e[3]
    od, os_ = HALF * (o[1] - o[3]), HALF * (o[1] + o[3])
    pairs = [
        (o[0] + od, o[2] + os_),
        (e[0] - e[2], e[1] - e[3]),
        (o[0] - od, os_ - o[2]),
    ]
    u = []
    for i, x in enumerate((e02 + e13, e02 - e13)):
        coef = dot(1, i, halves(x))
        u.append(dot(2, i, keep(coef, class_modes(4 * i, 4 * i))))
    su, du = u[0] + u[1], u[0] - u[1]
    uv = []
    for i, x in enumerate(pairs):
        coef = dot(0, i, halves(jnp.concatenate(x, axis=0)))
        p = i + 1
        r = dot(1, 2 + i, keep(coef, class_modes(p, SEG - p, p, SEG - p)))
        uv.append((r[:LOC], r[LOC:]))
    (u1, v1), (u2, v2), (u3, v3) = uv
    p = [su + u2, du + v2, su - u2, du - v2]
    d13, s13 = HALF * (u1 - u3), HALF * (v1 + v3)
    q = [u1 + u3, s13 + d13, v1 - v3, s13 - d13]
    return [p[i] + q[i] for i in range(4)] + [p[i] - q[i] for i in range(4)]


def run(copies):
    for c in copies:
        c.start()
    for c in copies:
        c.wait()


def gather_kernel(role_ref, x_ref, *refs):
    sent, (o_ref, sem) = refs[:SEG], refs[SEG:]

    @pl.when(role_ref[0] == 1)
    def _():
        for d in range(SEG):
            sent[d][...] = x_ref[STAY + lax.rem(role_ref[1] + d, SEG)]

    @pl.when(role_ref[0] != 1)
    def _():
        run([pltpu.make_async_copy(x_ref, o_ref, sem)])


def filter_kernel(role_ref, lines_ref, *refs):
    got, (counts_ref, *tables), refs = refs[:SEG], refs[SEG : SEG + 4], refs[SEG + 4 :]
    stay_ref, back, turned = refs[0], refs[1 : SEG + 1], refs[SEG + 1]
    counts = counts_ref[...]

    @pl.when(role_ref[0] == 1)
    def _():
        for i in range(2):
            done = filter_lines([lines_ref[s, i] for s in range(SEG)], counts, tables)
            for s in range(SEG):
                stay_ref[s, i] = done[s]

    @pl.when(role_ref[0] == 2)
    def _():
        for d in range(SEG):
            turned[lax.rem(role_ref[1] + SEG - d, SEG)] = got[d][...]
        done = filter_lines([turned[s] for s in range(SEG)], counts, tables)
        for s in range(SEG):
            turned[s] = done[s]
        for d in range(SEG):
            back[d][...] = turned[lax.rem(role_ref[1] + SEG - d, SEG)]


def finish_kernel(role_ref, base_ref, stay_ref, *refs):
    home, o_ref, sem = refs[:SEG], refs[SEG], refs[SEG + 1]
    del base_ref

    @pl.when(role_ref[0] == 1)
    def _():
        copies = [pltpu.make_async_copy(stay_ref, o_ref.at[pl.ds(0, STAY)], sem.at[SEG])]
        for d in range(SEG):
            group = STAY + lax.rem(role_ref[1] + d, SEG)
            copies.append(pltpu.make_async_copy(home[d], o_ref.at[group], sem.at[d]))
        run(copies)


def solution(mesh):
    n_phi, n_theta, n_row = (mesh.shape[a] for a in ("phi", "theta", "row"))
    last = n_theta - 1
    caps, helpers = (0, 1, last - 1, last), (2, 3, last - 3, last - 2)

    def at(z, t, r):
        return (z * n_theta + t) * n_row + r

    groups = [[at(z, t, r) for z in range(n_phi)] for t in caps for r in range(n_row)]
    for t in range(2, last - 1, 2):
        for z in range(n_phi):
            groups.append([at(z, t + c, r) for r in range(n_row) for c in range(2)])

    def pairs(sources, targets, d):
        return [
            (z * n_theta + a, (z + d) % n_phi * n_theta + b)
            for z in range(n_phi)
            for a, b in zip(sources, targets)
        ]

    def shift(v, sources, targets, d):
        return lax.ppermute(v, ("phi", "theta"), pairs(sources, targets, d))

    smem, vmem, either = (pl.BlockSpec(memory_space=m) for m in (pltpu.SMEM, pltpu.VMEM, pl.ANY))
    small = pltpu.CompilerParams(vmem_limit_bytes=16 << 20)

    def exchange(v):
        return lax.all_to_all(
            v,
            ("phi", "theta", "row"),
            split_axis=0,
            concat_axis=0,
            tiled=True,
            axis_index_groups=groups,
        )

    def on_device(fields, kept_counts):
        nf, shells, points, rows = fields.shape
        total = nf * shells
        theta, z = lax.axis_index("theta"), lax.axis_index("phi")
        is_cap = (theta < 2) | (theta > last - 2)
        is_helper = ((theta >= 2) & (theta < 4)) | ((theta > last - 4) & (theta <= last - 2))
        role = jnp.stack([jnp.where(is_cap, 1, jnp.where(is_helper, 2, 0)), z]).astype(jnp.int32)
        band = jnp.bitwise_and(theta, 1) + jnp.where(theta < n_theta // 2, 0, 2)
        counts = lax.dynamic_slice(kept_counts, (band * rows,), (rows,)).reshape(1, rows)
        x = fields.reshape(total, points, rows)
        one = jax.ShapeDtypeStruct((points, rows), jnp.float32)
        lines = exchange(x[:STAY])
        *sent, base = pl.pallas_call(
            gather_kernel,
            out_shape=[one] * SEG + [jax.ShapeDtypeStruct(x.shape, x.dtype)],
            in_specs=[smem, vmem],
            out_specs=[vmem] * SEG + [either],
            scratch_shapes=[pltpu.SemaphoreType.DMA],
            compiler_params=small,
            name="gather_groups",
        )(role, x)
        got = [None] * SEG
        for d in FAR + NEAR:
            got[d] = shift(sent[d], caps, helpers, d)
        stay, *back = pl.pallas_call(
            filter_kernel,
            out_shape=[jax.ShapeDtypeStruct((SEG, 2, points, rows), jnp.float32)] + [one] * SEG,
            in_specs=[smem] + [vmem] * (SEG + 5),
            out_specs=[vmem] * (SEG + 1),
            scratch_shapes=[pltpu.VMEM((SEG, points, rows), jnp.float32)],
            compiler_params=small,
            name="filter_lines",
        )(role, lines.reshape(SEG, 2, points, rows), *got, counts, *[jnp.asarray(t) for t in TABLES])
        stay = exchange(stay.reshape(STAY, points, rows))
        home = [None] * SEG
        along = {d: shift(back[d], helpers, helpers, -d) for d in FAR}
        for d in NEAR:
            home[d] = shift(back[d], helpers, caps, -d)
        for d in FAR:
            home[d] = shift(along[d], helpers, caps, 0)
        out = pl.pallas_call(
            finish_kernel,
            out_shape=jax.ShapeDtypeStruct(x.shape, x.dtype),
            in_specs=[smem, either] + [vmem] * (SEG + 1),
            out_specs=either,
            scratch_shapes=[pltpu.SemaphoreType.DMA((SEG + 1,))],
            input_output_aliases={1: 0},
            compiler_params=small,
            name="finish",
        )(role, base, stay, *home)
        return out.reshape(fields.shape)

    return jax.shard_map(
        on_device,
        mesh=mesh,
        in_specs=(P(None, "row", "phi", "theta"), P()),
        out_specs=P(None, "row", "phi", "theta"),
        check_vma=False,
    )
```

```python
import math

import jax
import jax.numpy as jnp
import numpy as np
from jax import lax
from jax.experimental import pallas as pl
from jax.experimental.pallas import tpu as pltpu
from jax.sharding import PartitionSpec as P

KMAX = 384
NPHI = 1536
SEG = 8
LOC = NPHI // SEG
MODES = KMAX // SEG
HALF = math.sqrt(0.5)


def cos_sin(k):
    turns = (k[:, None] * np.arange(LOC)[None, :]) % NPHI
    angle = turns * (2.0 * math.pi / NPHI)
    return np.cos(angle), np.sin(angle)


def matrices():
    m = SEG * np.arange(MODES)
    real = [np.concatenate(cos_sin(k)) for k in (m, m + 4)]
    paired = []
    for p in (1, 2, 3):
        cp, sp = cos_sin(m + p)
        cn, sn = cos_sin(m + SEG - p)
        paired.append(np.block([[cp, -sp], [cn, sn], [sp, cp], [sn, -cn]]))
    return paired, real + [a.T for a in paired], [a.T for a in real]


def stacked(group):
    parts = []
    for m in group:
        high = m.astype(jnp.bfloat16)
        parts += [high, (m - high.astype(np.float64)).astype(jnp.bfloat16)]
    return np.concatenate(parts)


TABLES = [stacked(g) for g in matrices()]
PLACES = [[2 * sum(m.shape[0] for m in g[:i]) for i in range(len(g) + 1)] for g in matrices()]
STAY = 2 * SEG
FARTHEST_FIRST = (4, 3, 5, 2, 6, 1, 7, 0)


def halves(x):
    high = x.astype(jnp.bfloat16)
    low = (x - high.astype(jnp.float32)).astype(jnp.bfloat16)
    return jnp.concatenate([high, low], axis=1)


def quarters(r):
    n, c = r.shape[0] // 2, r.shape[1] // 2
    return r[:n, :c] + (r[:n, c:] + r[n:, :c] + r[n:, c:])


def class_modes(*offsets):
    m = SEG * lax.broadcasted_iota(jnp.int32, (MODES, 128), 0)
    return jnp.concatenate([m + p for p in offsets], axis=0)


def filter_lines(y, counts, tables):
    def dot(g, i, x):
        rows = tables[g][PLACES[g][i] : PLACES[g][i + 1], :]
        return quarters(lax.dot_general(rows, x, (((1,), (0,)), ((), ())), preferred_element_type=jnp.float32))

    def keep(coef, k):
        weight = jnp.where(k == 0, 1.0 / NPHI, 2.0 / NPHI)
        return halves(jnp.where(k < counts, coef * weight, 0.0))

    e = [y[i] + y[i + 4] for i in range(4)]
    o = [y[i] - y[i + 4] for i in range(4)]
    e02, e13 = e[0] + e[2], e[1] + e[3]
    od, os_ = HALF * (o[1] - o[3]), HALF * (o[1] + o[3])
    pairs = [
        (o[0] + od, o[2] + os_),
        (e[0] - e[2], e[1] - e[3]),
        (o[0] - od, os_ - o[2]),
    ]
    u = []
    for i, x in enumerate((e02 + e13, e02 - e13)):
        coef = dot(1, i, halves(x))
        u.append(dot(2, i, keep(coef, class_modes(4 * i, 4 * i))))
    su, du = u[0] + u[1], u[0] - u[1]
    uv = []
    for i, x in enumerate(pairs):
        coef = dot(0, i, halves(jnp.concatenate(x, axis=0)))
        p = i + 1
        r = dot(1, 2 + i, keep(coef, class_modes(p, SEG - p, p, SEG - p)))
        uv.append((r[:LOC], r[LOC:]))
    (u1, v1), (u2, v2), (u3, v3) = uv
    p = [su + u2, du + v2, su - u2, du - v2]
    d13, s13 = HALF * (u1 - u3), HALF * (v1 + v3)
    q = [u1 + u3, s13 + d13, v1 - v3, s13 - d13]
    return [p[i] + q[i] for i in range(4)] + [p[i] - q[i] for i in range(4)]


def run(copies):
    for c in copies:
        c.start()
    for c in copies:
        c.wait()


def gather_kernel(role_ref, x_ref, *refs):
    sent, (o_ref, sem) = refs[:SEG], refs[SEG:]

    @pl.when(role_ref[0] == 1)
    def _():
        for d in range(SEG):
            sent[d][...] = x_ref[STAY + lax.rem(role_ref[1] + d, SEG)]

    @pl.when(role_ref[0] != 1)
    def _():
        run([pltpu.make_async_copy(x_ref, o_ref, sem)])


def filter_kernel(role_ref, lines_ref, *refs):
    got, (counts_ref, *tables), refs = refs[:SEG], refs[SEG : SEG + 4], refs[SEG + 4 :]
    stay_ref, back, turned = refs[0], refs[1 : SEG + 1], refs[SEG + 1]
    counts = counts_ref[...]

    @pl.when(role_ref[0] == 1)
    def _():
        done = filter_lines([lines_ref[s] for s in range(SEG)], counts, tables)
        for s in range(SEG):
            stay_ref[s] = done[s]

    @pl.when((role_ref[0] == 2) & (pl.program_id(0) == 0))
    def _():
        for d in range(SEG):
            turned[lax.rem(role_ref[1] + SEG - d, SEG)] = got[d][...]
        done = filter_lines([turned[s] for s in range(SEG)], counts, tables)
        for s in range(SEG):
            turned[s] = done[s]
        for d in range(SEG):
            back[d][...] = turned[lax.rem(role_ref[1] + SEG - d, SEG)]


def finish_kernel(role_ref, base_ref, stay_ref, *refs):
    home, o_ref, sem = refs[:SEG], refs[SEG], refs[SEG + 1]
    del base_ref

    @pl.when(role_ref[0] == 1)
    def _():
        copies = [pltpu.make_async_copy(stay_ref, o_ref.at[pl.ds(0, STAY)], sem.at[SEG])]
        for d in range(SEG):
            group = STAY + lax.rem(role_ref[1] + d, SEG)
            copies.append(pltpu.make_async_copy(home[d], o_ref.at[group], sem.at[d]))
        run(copies)


def solution(mesh):
    n_phi, n_theta, n_row = (mesh.shape[a] for a in ("phi", "theta", "row"))
    last = n_theta - 1
    caps, helpers, relays = ((a, a + 1, last - 1 - a, last - a) for a in (0, 2, 4))

    def at(z, t, r):
        return (z * n_theta + t) * n_row + r

    groups = [[at(z, t, r) for z in range(n_phi)] for t in caps for r in range(n_row)]
    for t in range(2, last - 1, 2):
        for z in range(n_phi):
            groups.append([at(z, t + c, r) for r in range(n_row) for c in range(2)])

    def pairs(sources, targets, d):
        return [
            (z * n_theta + a, (z + d) % n_phi * n_theta + b)
            for z in range(n_phi)
            for a, b in zip(sources, targets)
        ]

    def shift(v, sources, targets, d):
        return lax.ppermute(v, ("phi", "theta"), pairs(sources, targets, d))

    smem, vmem, either = (pl.BlockSpec(memory_space=m) for m in (pltpu.SMEM, pltpu.VMEM, pl.ANY))
    small = pltpu.CompilerParams(vmem_limit_bytes=16 << 20)

    def exchange(v):
        return lax.all_to_all(
            v,
            ("phi", "theta", "row"),
            split_axis=0,
            concat_axis=0,
            tiled=True,
            axis_index_groups=groups,
        )

    def on_device(fields, kept_counts):
        nf, shells, points, rows = fields.shape
        total = nf * shells
        theta, z = lax.axis_index("theta"), lax.axis_index("phi")
        is_cap = (theta < 2) | (theta > last - 2)
        is_helper = ((theta >= 2) & (theta < 4)) | ((theta > last - 4) & (theta <= last - 2))
        role = jnp.stack([jnp.where(is_cap, 1, jnp.where(is_helper, 2, 0)), z]).astype(jnp.int32)
        band = jnp.bitwise_and(theta, 1) + jnp.where(theta < n_theta // 2, 0, 2)
        counts = lax.dynamic_slice(kept_counts, (band * rows,), (rows,)).reshape(1, rows)
        x = fields.reshape(total, points, rows)
        one = jax.ShapeDtypeStruct((points, rows), jnp.float32)
        lines = exchange(x[:STAY])
        *sent, base = pl.pallas_call(
            gather_kernel,
            out_shape=[one] * SEG + [jax.ShapeDtypeStruct(x.shape, x.dtype)],
            in_specs=[smem, vmem],
            out_specs=[vmem] * SEG + [either],
            scratch_shapes=[pltpu.SemaphoreType.DMA],
            compiler_params=small,
            name="gather_groups",
        )(role, x)
        got = [None] * SEG
        for d in FARTHEST_FIRST:
            got[d] = shift(sent[d], caps, helpers, d)
        one_set = pl.BlockSpec((SEG, None, points, rows), lambda i: (0, i, 0, 0))
        stay, *back = pl.pallas_call(
            filter_kernel,
            out_shape=[jax.ShapeDtypeStruct((SEG, 2, points, rows), jnp.float32)] + [one] * SEG,
            grid=(2,),
            in_specs=[smem, one_set] + [vmem] * (SEG + 4),
            out_specs=[one_set] + [vmem] * SEG,
            scratch_shapes=[pltpu.VMEM((SEG, points, rows), jnp.float32)],
            compiler_params=small,
            name="filter_lines",
        )(role, lines.reshape(SEG, 2, points, rows), *got, counts, *[jnp.asarray(t) for t in TABLES])
        stay = exchange(stay.reshape(STAY, points, rows))
        home = [None] * SEG
        relayed = {d: shift(back[d], helpers, relays, -d) for d in FARTHEST_FIRST[:-1]}
        home[0] = shift(back[0], helpers, caps, 0)
        for d, v in relayed.items():
            home[d] = shift(v, relays, caps, 0)
        out = pl.pallas_call(
            finish_kernel,
            out_shape=jax.ShapeDtypeStruct(x.shape, x.dtype),
            in_specs=[smem, either] + [vmem] * (SEG + 1),
            out_specs=either,
            scratch_shapes=[pltpu.SemaphoreType.DMA((SEG + 1,))],
            input_output_aliases={1: 0},
            compiler_params=small,
            name="finish",
        )(role, base, stay, *home)
        return out.reshape(fields.shape)

    return jax.shard_map(
        on_device,
        mesh=mesh,
        in_specs=(P(None, "row", "phi", "theta"), P()),
        out_specs=P(None, "row", "phi", "theta"),
        check_vma=False,
    )
```

```python
import math

import jax
import jax.numpy as jnp
import numpy as np
from jax import lax
from jax.experimental import pallas as pl
from jax.experimental.pallas import tpu as pltpu
from jax.sharding import PartitionSpec as P

KMAX = 384
NPHI = 1536
SEG = 8
LOC = NPHI // SEG
MODES = KMAX // SEG
HALF = math.sqrt(0.5)


def cos_sin(k):
    turns = (k[:, None] * np.arange(LOC)[None, :]) % NPHI
    angle = turns * (2.0 * math.pi / NPHI)
    return np.cos(angle), np.sin(angle)


def matrices():
    m = SEG * np.arange(MODES)
    real = [np.concatenate(cos_sin(k)) for k in (m, m + 4)]
    paired = []
    for p in (1, 2, 3):
        cp, sp = cos_sin(m + p)
        cn, sn = cos_sin(m + SEG - p)
        paired.append(np.block([[cp, -sp], [cn, sn], [sp, cp], [sn, -cn]]))
    return real, paired


def parts(m):
    high = m.astype(jnp.bfloat16)
    return high, (m - high.astype(np.float64)).astype(jnp.bfloat16)


def table():
    real, paired = matrices()
    blocks, places, at = [], {}, 0

    def put(*columns):
        nonlocal at
        left = 0
        for key, m in columns:
            places.setdefault(key, []).append((at, m.shape[0], left, m.shape[1]))
            left += m.shape[1]
        blocks.append(np.concatenate([m for _, m in columns], axis=1))
        at += blocks[-1].shape[0]

    for i, m in enumerate(paired):
        for part in parts(m):
            put((("analysis", i + 2), part))
    back = [parts(m.T) for m in paired]
    for n in range(2):
        put((("synthesis", 2), back[0][n]), (("synthesis", 3), back[1][n]))
    put((("synthesis", 4), back[2][0]), (("synthesis", 4), back[2][1]))
    ahead = [parts(m) for m in real]
    for n in range(2):
        put((("analysis", 0), ahead[0][n]), (("analysis", 1), ahead[1][n]))
    put(*((("synthesis", i), part) for i in range(2) for part in parts(real[i].T)))
    return np.concatenate(blocks), places


TABLE, PLACES = table()
PACK = LOC // 2
SIZE = LOC + PACK
HOME = SEG + SEG // 2
FAR = (4, 3, 5, 2, 6)
NEAR = (0, 1, 7)


def halves(x):
    high = x.astype(jnp.bfloat16)
    low = (x - high.astype(jnp.float32)).astype(jnp.bfloat16)
    return jnp.concatenate([high, low], axis=1)


def quarters(r):
    n, c = r.shape[0] // 2, r.shape[1] // 2
    return r[:n, :c] + (r[:n, c:] + r[n:, :c] + r[n:, c:])


def class_modes(*offsets):
    m = SEG * lax.broadcasted_iota(jnp.int32, (MODES, 128), 0)
    return jnp.concatenate([m + p for p in offsets], axis=0)


def filter_lines(y, counts, table_ref):
    def dot(key, i, x):
        rows = [table_ref[r : r + n, c : c + w] for r, n, c, w in PLACES[key, i]]
        rows = jnp.concatenate(rows, axis=0)
        return quarters(lax.dot_general(rows, x, (((1,), (0,)), ((), ())), preferred_element_type=jnp.float32))

    def keep(coef, k):
        weight = jnp.where(k == 0, 1.0 / NPHI, 2.0 / NPHI)
        return halves(jnp.where(k < counts, coef * weight, 0.0))

    e = [y[i] + y[i + 4] for i in range(4)]
    o = [y[i] - y[i + 4] for i in range(4)]
    e02, e13 = e[0] + e[2], e[1] + e[3]
    od, os_ = HALF * (o[1] - o[3]), HALF * (o[1] + o[3])
    pairs = [
        (o[0] + od, o[2] + os_),
        (e[0] - e[2], e[1] - e[3]),
        (o[0] - od, os_ - o[2]),
    ]
    u = []
    for i, x in enumerate((e02 + e13, e02 - e13)):
        coef = dot("analysis", i, halves(x))
        u.append(dot("synthesis", i, keep(coef, class_modes(4 * i, 4 * i))))
    su, du = u[0] + u[1], u[0] - u[1]
    uv = []
    for i, x in enumerate(pairs):
        coef = dot("analysis", i + 2, halves(jnp.concatenate(x, axis=0)))
        p = i + 1
        r = dot("synthesis", i + 2, keep(coef, class_modes(p, SEG - p, p, SEG - p)))
        uv.append((r[:LOC], r[LOC:]))
    (u1, v1), (u2, v2), (u3, v3) = uv
    p = [su + u2, du + v2, su - u2, du - v2]
    d13, s13 = HALF * (u1 - u3), HALF * (v1 + v3)
    q = [u1 + u3, s13 + d13, v1 - v3, s13 - d13]
    return [p[i] + q[i] for i in range(4)] + [p[i] - q[i] for i in range(4)]


def swap(v):
    return pltpu.roll(v, 64, 1)


def low_lanes():
    return lax.broadcasted_iota(jnp.int32, (PACK, 128), 1) < 64


def pack(v, half):
    top, bottom = v[:PACK], v[PACK:]
    if half:
        return jnp.where(low_lanes(), swap(top), bottom)
    return jnp.where(low_lanes(), top, swap(bottom))


def unpack(even, odd):
    return jnp.where(low_lanes(), even, swap(odd)), jnp.where(low_lanes(), swap(even), odd)


def run(copies):
    for c in copies:
        c.start()
    for c in copies:
        c.wait()


def stay_kernel(role_ref, x_ref, o_ref):
    @pl.when(role_ref[0] == 1)
    def _():
        for z in range(SEG):
            o_ref[z, :LOC] = x_ref[z]
            o_ref[z, LOC:] = pack(x_ref[SEG + z // 2], z % 2)


def leave_kernel(role_ref, x_ref, *refs):
    sent, (o_ref, packed, sem) = refs[:SEG], refs[SEG:]

    @pl.when(role_ref[0] == 1)
    def _():
        for z in range(SEG):
            packed[z] = pack(x_ref[HOME + SEG + z // 2], z % 2)
        for d in range(SEG):
            z = lax.rem(role_ref[1] + d, SEG)
            sent[d][:LOC] = x_ref[HOME + z]
            sent[d][LOC:] = packed[z]

    @pl.when(role_ref[0] != 1)
    def _():
        run([pltpu.make_async_copy(x_ref, o_ref, sem)])


def filter_kernel(role_ref, lines_ref, *refs):
    got, (counts_ref, table_ref), refs = refs[:SEG], refs[SEG : SEG + 2], refs[SEG + 2 :]
    stay_ref, back, turned = refs[0], refs[1 : SEG + 1], refs[SEG + 1]

    def apply(source, target):
        done = filter_lines([source[s, :LOC] for s in range(SEG)], counts_ref[0:1], table_ref)
        for s in range(SEG):
            target[s, :LOC] = done[s]
        half = [source[s, LOC:] for s in range(SEG)]
        half = [jnp.concatenate([v, swap(v)], axis=0) for v in half]
        done = filter_lines(half, counts_ref[1:2], table_ref)
        for s in range(SEG):
            target[s, LOC:] = pack(done[s], 0)

    @pl.when(role_ref[0] == 1)
    def _():
        apply(lines_ref, stay_ref)

    @pl.when(role_ref[0] == 2)
    def _():
        for d in range(SEG):
            turned[lax.rem(role_ref[1] + SEG - d, SEG)] = got[d][...]
        apply(turned, turned)
        for d in range(SEG):
            back[d][...] = turned[lax.rem(role_ref[1] + SEG - d, SEG)]


def finish_kernel(role_ref, base_ref, stay_ref, *refs):
    home, (o_ref, packed, whole, sem) = refs[:SEG], refs[SEG:]
    del base_ref

    @pl.when(role_ref[0] == 1)
    def _():
        copies = []
        for z in range(SEG):
            copies.append(pltpu.make_async_copy(stay_ref.at[z, pl.ds(0, LOC)], o_ref.at[z], sem.at[z]))
        for d in range(SEG):
            z = lax.rem(role_ref[1] + d, SEG)
            source = home[d].at[pl.ds(0, LOC)]
            copies.append(pltpu.make_async_copy(source, o_ref.at[HOME + z], sem.at[SEG + d]))
        for c in copies:
            c.start()
        for d in range(SEG):
            packed[lax.rem(role_ref[1] + d, SEG)] = home[d][LOC:]
        for i in range(SEG // 2):
            for n, (even, odd) in enumerate(
                (
                    (stay_ref[2 * i, LOC:], stay_ref[2 * i + 1, LOC:]),
                    (packed[2 * i], packed[2 * i + 1]),
                )
            ):
                top, bottom = unpack(even, odd)
                whole[n, i, :PACK] = top
                whole[n, i, PACK:] = bottom
        last = []
        for n, first in enumerate((SEG, HOME + SEG)):
            target = o_ref.at[pl.ds(first, SEG // 2)]
            last.append(pltpu.make_async_copy(whole.at[n], target, sem.at[2 * SEG + n]))
        for c in last:
            c.start()
        for c in copies + last:
            c.wait()


def solution(mesh):
    n_phi, n_theta, n_row = (mesh.shape[a] for a in ("phi", "theta", "row"))
    last = n_theta - 1
    caps, helpers, relays = ((a, a + 1, last - 1 - a, last - a) for a in (0, 2, 4))

    def at(z, t, r):
        return (z * n_theta + t) * n_row + r

    groups = [[at(z, t, r) for z in range(n_phi)] for t in caps for r in range(n_row)]
    for t in range(2, last - 1, 2):
        for z in range(n_phi):
            groups.append([at(z, t + c, r) for r in range(n_row) for c in range(2)])

    def pairs(sources, targets, d):
        return [
            (z * n_theta + a, (z + d) % n_phi * n_theta + b)
            for z in range(n_phi)
            for a, b in zip(sources, targets)
        ]

    def shift(v, sources, targets, d):
        return lax.ppermute(v, ("phi", "theta"), pairs(sources, targets, d))

    smem, vmem, either = (pl.BlockSpec(memory_space=m) for m in (pltpu.SMEM, pltpu.VMEM, pl.ANY))
    small = pltpu.CompilerParams(vmem_limit_bytes=16 << 20)

    def exchange(v):
        return lax.all_to_all(
            v,
            ("phi", "theta", "row"),
            split_axis=0,
            concat_axis=0,
            tiled=True,
            axis_index_groups=groups,
        )

    def on_device(fields, kept_counts):
        nf, shells, points, rows = fields.shape
        total = nf * shells
        theta, z = lax.axis_index("theta"), lax.axis_index("phi")
        is_cap = (theta < 2) | (theta > last - 2)
        is_helper = ((theta >= 2) & (theta < 4)) | ((theta > last - 4) & (theta <= last - 2))
        role = jnp.stack([jnp.where(is_cap, 1, jnp.where(is_helper, 2, 0)), z]).astype(jnp.int32)
        band = jnp.bitwise_and(theta, 1) + jnp.where(theta < n_theta // 2, 0, 2)
        counts = lax.dynamic_slice(kept_counts, (band * rows,), (rows,)).reshape(1, rows)
        x = fields.reshape(total, points, rows)
        kinds = jnp.concatenate([counts, jnp.where(z % 2 == 0, counts, jnp.roll(counts, 64, axis=1))])
        one = jax.ShapeDtypeStruct((SIZE, rows), jnp.float32)
        all_of = jax.ShapeDtypeStruct((SEG, SIZE, rows), jnp.float32)
        kept = pl.pallas_call(
            stay_kernel,
            out_shape=all_of,
            in_specs=[smem, vmem],
            out_specs=vmem,
            compiler_params=small,
            name="stay",
        )(role, x)
        lines = exchange(kept)
        *sent, base = pl.pallas_call(
            leave_kernel,
            out_shape=[one] * SEG + [jax.ShapeDtypeStruct(x.shape, x.dtype)],
            in_specs=[smem, vmem],
            out_specs=[vmem] * SEG + [either],
            scratch_shapes=[pltpu.VMEM((SEG, PACK, rows), jnp.float32), pltpu.SemaphoreType.DMA],
            compiler_params=small,
            name="leave",
        )(role, x)
        held = jnp.asarray(TABLE)
        got = [None] * SEG
        for d in FAR + NEAR:
            got[d] = shift(sent[d], caps, helpers, d)
        stay, *back = pl.pallas_call(
            filter_kernel,
            out_shape=[all_of] + [one] * SEG,
            in_specs=[smem] + [vmem] * (SEG + 3),
            out_specs=[vmem] * (SEG + 1),
            scratch_shapes=[pltpu.VMEM(all_of.shape, jnp.float32)],
            compiler_params=small,
            name="filter_lines",
        )(role, lines, *got, kinds, held)
        stay = exchange(stay)
        home, relayed = [None] * SEG, {}
        for far, near in zip(FAR, NEAR + (None,) * 2):
            relayed[far] = shift(back[far], helpers, relays, -far)
            if near is not None:
                home[near] = shift(back[near], helpers, caps, -near)
        for d in FAR:
            home[d] = shift(relayed[d], relays, caps, 0)
        out = pl.pallas_call(
            finish_kernel,
            out_shape=jax.ShapeDtypeStruct(x.shape, x.dtype),
            in_specs=[smem, either] + [vmem] * (SEG + 1),
            out_specs=either,
            scratch_shapes=[
                pltpu.VMEM((SEG, PACK, rows), jnp.float32),
                pltpu.VMEM((2, SEG // 2, points, rows), jnp.float32),
                pltpu.SemaphoreType.DMA((2 * SEG + 2,)),
            ],
            input_output_aliases={1: 0},
            compiler_params=small,
            name="finish",
        )(role, base, stay, *home)
        return out.reshape(fields.shape)

    return jax.shard_map(
        on_device,
        mesh=mesh,
        in_specs=(P(None, "row", "phi", "theta"), P()),
        out_specs=P(None, "row", "phi", "theta"),
        check_vma=False,
    )
```

```python
import math

import jax
import jax.numpy as jnp
import numpy as np
from jax import lax
from jax.experimental import pallas as pl
from jax.experimental.pallas import tpu as pltpu
from jax.sharding import PartitionSpec as P

KMAX = 384
NPHI = 1536
SEG = 8
LOC = NPHI // SEG
MODES = KMAX // SEG
HALF = math.sqrt(0.5)


def cos_sin(k):
    turns = (k[:, None] * np.arange(LOC)[None, :]) % NPHI
    angle = turns * (2.0 * math.pi / NPHI)
    return np.cos(angle), np.sin(angle)


def matrices():
    m = SEG * np.arange(MODES)
    real = [np.concatenate(cos_sin(k)) for k in (m, m + 4)]
    paired = []
    for p in (1, 2, 3):
        cp, sp = cos_sin(m + p)
        cn, sn = cos_sin(m + SEG - p)
        paired.append(np.block([[cp, -sp], [cn, sn], [sp, cp], [sn, -cn]]))
    return real, paired


def parts(m):
    high = m.astype(jnp.bfloat16)
    return high, (m - high.astype(np.float64)).astype(jnp.bfloat16)


def table():
    real, paired = matrices()
    blocks, places, at = [], {}, 0

    def put(*columns):
        nonlocal at
        left = 0
        for key, m in columns:
            places.setdefault(key, []).append((at, m.shape[0], left, m.shape[1]))
            left += m.shape[1]
        blocks.append(np.concatenate([m for _, m in columns], axis=1))
        at += blocks[-1].shape[0]

    for i, m in enumerate(paired):
        for part in parts(m):
            put((("analysis", i + 2), part))
    back = [parts(m.T) for m in paired]
    for n in range(2):
        put((("synthesis", 2), back[0][n]), (("synthesis", 3), back[1][n]))
    put((("synthesis", 4), back[2][0]), (("synthesis", 4), back[2][1]))
    ahead = [parts(m) for m in real]
    for n in range(2):
        put((("analysis", 0), ahead[0][n]), (("analysis", 1), ahead[1][n]))
    put(*((("synthesis", i), part) for i in range(2) for part in parts(real[i].T)))
    return np.concatenate(blocks), places


TABLE, PLACES = table()
PACK = LOC // 2
SIZE = LOC + PACK
HOME = SEG + SEG // 2
FAR = (4, 3, 5, 2, 6)
OUT = (4, 3, 5, 2, 6, 1, 7, 0)
BACK = (4, 0, 3, 5, 1, 2, 7, 6)


def halves(x):
    high = x.astype(jnp.bfloat16)
    low = (x - high.astype(jnp.float32)).astype(jnp.bfloat16)
    return jnp.concatenate([high, low], axis=1)


def quarters(r):
    n, c = r.shape[0] // 2, r.shape[1] // 2
    return r[:n, :c] + (r[:n, c:] + r[n:, :c] + r[n:, c:])


def class_modes(*offsets):
    m = SEG * lax.broadcasted_iota(jnp.int32, (MODES, 128), 0)
    return jnp.concatenate([m + p for p in offsets], axis=0)


def filter_lines(y, counts, table_ref):
    def dot(key, i, x):
        rows = [table_ref[r : r + n, c : c + w] for r, n, c, w in PLACES[key, i]]
        rows = jnp.concatenate(rows, axis=0)
        return quarters(lax.dot_general(rows, x, (((1,), (0,)), ((), ())), preferred_element_type=jnp.float32))

    def keep(coef, k):
        weight = jnp.where(k == 0, 1.0 / NPHI, 2.0 / NPHI)
        return halves(jnp.where(k < counts, coef * weight, 0.0))

    e = [y[i] + y[i + 4] for i in range(4)]
    o = [y[i] - y[i + 4] for i in range(4)]
    e02, e13 = e[0] + e[2], e[1] + e[3]
    od, os_ = HALF * (o[1] - o[3]), HALF * (o[1] + o[3])
    pairs = [
        (o[0] + od, o[2] + os_),
        (e[0] - e[2], e[1] - e[3]),
        (o[0] - od, os_ - o[2]),
    ]
    u = []
    for i, x in enumerate((e02 + e13, e02 - e13)):
        coef = dot("analysis", i, halves(x))
        u.append(dot("synthesis", i, keep(coef, class_modes(4 * i, 4 * i))))
    su, du = u[0] + u[1], u[0] - u[1]
    uv = []
    for i, x in enumerate(pairs):
        coef = dot("analysis", i + 2, halves(jnp.concatenate(x, axis=0)))
        p = i + 1
        r = dot("synthesis", i + 2, keep(coef, class_modes(p, SEG - p, p, SEG - p)))
        uv.append((r[:LOC], r[LOC:]))
    (u1, v1), (u2, v2), (u3, v3) = uv
    p = [su + u2, du + v2, su - u2, du - v2]
    d13, s13 = HALF * (u1 - u3), HALF * (v1 + v3)
    q = [u1 + u3, s13 + d13, v1 - v3, s13 - d13]
    return [p[i] + q[i] for i in range(4)] + [p[i] - q[i] for i in range(4)]


def swap(v):
    return pltpu.roll(v, 64, 1)


def low_lanes():
    return lax.broadcasted_iota(jnp.int32, (PACK, 128), 1) < 64


def pack(v, half):
    top, bottom = v[:PACK], v[PACK:]
    if half:
        return jnp.where(low_lanes(), swap(top), bottom)
    return jnp.where(low_lanes(), top, swap(bottom))


def unpack(even, odd):
    return jnp.where(low_lanes(), even, swap(odd)), jnp.where(low_lanes(), swap(even), odd)


def run(copies):
    for c in copies:
        c.start()
    for c in copies:
        c.wait()


def stay_kernel(role_ref, x_ref, o_ref):
    @pl.when(role_ref[0] == 1)
    def _():
        for z in range(SEG):
            o_ref[z, :LOC] = x_ref[z]
            o_ref[z, LOC:] = pack(x_ref[SEG + z // 2], z % 2)


def leave_kernel(role_ref, x_ref, *refs):
    sent, (o_ref, packed, sem) = refs[:SEG], refs[SEG:]

    @pl.when(role_ref[0] == 1)
    def _():
        for z in range(SEG):
            packed[z] = pack(x_ref[HOME + SEG + z // 2], z % 2)
        for sent_ref, d in zip(sent, OUT):
            z = lax.rem(role_ref[1] + d, SEG)
            sent_ref[:LOC] = x_ref[HOME + z]
            sent_ref[LOC:] = packed[z]

    @pl.when(role_ref[0] != 1)
    def _():
        run([pltpu.make_async_copy(x_ref, o_ref, sem)])


def filter_kernel(role_ref, lines_ref, *refs):
    got, (counts_ref, table_ref), refs = refs[:SEG], refs[SEG : SEG + 2], refs[SEG + 2 :]
    stay_ref, back, turned = refs[0], refs[1 : SEG + 1], refs[SEG + 1]

    def apply(source, target):
        done = filter_lines([source[s, :LOC] for s in range(SEG)], counts_ref[0:1], table_ref)
        for s in range(SEG):
            target[s, :LOC] = done[s]
        half = [source[s, LOC:] for s in range(SEG)]
        half = [jnp.concatenate([v, swap(v)], axis=0) for v in half]
        done = filter_lines(half, counts_ref[1:2], table_ref)
        for s in range(SEG):
            target[s, LOC:] = pack(done[s], 0)

    @pl.when(role_ref[0] == 1)
    def _():
        apply(lines_ref, stay_ref)

    @pl.when(role_ref[0] == 2)
    def _():
        for got_ref, d in zip(got, OUT):
            turned[lax.rem(role_ref[1] + SEG - d, SEG)] = got_ref[...]
        apply(turned, turned)
        for back_ref, d in zip(back, BACK):
            back_ref[...] = turned[lax.rem(role_ref[1] + SEG - d, SEG)]


def finish_kernel(role_ref, base_ref, stay_ref, *refs):
    home, (o_ref, packed, whole, sem) = refs[:SEG], refs[SEG:]
    del base_ref

    @pl.when(role_ref[0] == 1)
    def _():
        copies = []
        for z in range(SEG):
            copies.append(pltpu.make_async_copy(stay_ref.at[z, pl.ds(0, LOC)], o_ref.at[z], sem.at[z]))
        for d, home_ref in zip(BACK, home):
            z = lax.rem(role_ref[1] + d, SEG)
            source = home_ref.at[pl.ds(0, LOC)]
            copies.append(pltpu.make_async_copy(source, o_ref.at[HOME + z], sem.at[SEG + d]))
        for c in copies:
            c.start()
        for d, home_ref in zip(BACK, home):
            packed[lax.rem(role_ref[1] + d, SEG)] = home_ref[LOC:]
        for i in range(SEG // 2):
            for n, (even, odd) in enumerate(
                (
                    (stay_ref[2 * i, LOC:], stay_ref[2 * i + 1, LOC:]),
                    (packed[2 * i], packed[2 * i + 1]),
                )
            ):
                top, bottom = unpack(even, odd)
                whole[n, i, :PACK] = top
                whole[n, i, PACK:] = bottom
        last = []
        for n, first in enumerate((SEG, HOME + SEG)):
            target = o_ref.at[pl.ds(first, SEG // 2)]
            last.append(pltpu.make_async_copy(whole.at[n], target, sem.at[2 * SEG + n]))
        for c in last:
            c.start()
        for c in copies + last:
            c.wait()


def solution(mesh):
    n_phi, n_theta, n_row = (mesh.shape[a] for a in ("phi", "theta", "row"))
    last = n_theta - 1
    caps, helpers, relays = ((a, a + 1, last - 1 - a, last - a) for a in (0, 2, 4))

    def at(z, t, r):
        return (z * n_theta + t) * n_row + r

    groups = [[at(z, t, r) for z in range(n_phi)] for t in caps for r in range(n_row)]
    for t in range(2, last - 1, 2):
        for z in range(n_phi):
            groups.append([at(z, t + c, r) for r in range(n_row) for c in range(2)])

    def pairs(sources, targets, d):
        return [
            (z * n_theta + a, (z + d) % n_phi * n_theta + b)
            for z in range(n_phi)
            for a, b in zip(sources, targets)
        ]

    def shift(v, sources, targets, d):
        return lax.ppermute(v, ("phi", "theta"), pairs(sources, targets, d))

    smem, vmem, either = (pl.BlockSpec(memory_space=m) for m in (pltpu.SMEM, pltpu.VMEM, pl.ANY))
    small = pltpu.CompilerParams(vmem_limit_bytes=16 << 20)

    def exchange(v):
        return lax.all_to_all(
            v,
            ("phi", "theta", "row"),
            split_axis=0,
            concat_axis=0,
            tiled=True,
            axis_index_groups=groups,
        )

    def on_device(fields, kept_counts):
        nf, shells, points, rows = fields.shape
        total = nf * shells
        theta, z = lax.axis_index("theta"), lax.axis_index("phi")
        is_cap = (theta < 2) | (theta > last - 2)
        is_helper = ((theta >= 2) & (theta < 4)) | ((theta > last - 4) & (theta <= last - 2))
        role = jnp.stack([jnp.where(is_cap, 1, jnp.where(is_helper, 2, 0)), z]).astype(jnp.int32)
        band = jnp.bitwise_and(theta, 1) + jnp.where(theta < n_theta // 2, 0, 2)
        counts = lax.dynamic_slice(kept_counts, (band * rows,), (rows,)).reshape(1, rows)
        x = fields.reshape(total, points, rows)
        kinds = jnp.concatenate([counts, jnp.where(z % 2 == 0, counts, jnp.roll(counts, 64, axis=1))])
        one = jax.ShapeDtypeStruct((SIZE, rows), jnp.float32)
        all_of = jax.ShapeDtypeStruct((SEG, SIZE, rows), jnp.float32)
        kept = pl.pallas_call(
            stay_kernel,
            out_shape=all_of,
            in_specs=[smem, vmem],
            out_specs=vmem,
            compiler_params=small,
            name="stay",
        )(role, x)
        lines = exchange(kept)
        *sent, base = pl.pallas_call(
            leave_kernel,
            out_shape=[one] * SEG + [jax.ShapeDtypeStruct(x.shape, x.dtype)],
            in_specs=[smem, vmem],
            out_specs=[vmem] * SEG + [either],
            scratch_shapes=[pltpu.VMEM((SEG, PACK, rows), jnp.float32), pltpu.SemaphoreType.DMA],
            compiler_params=small,
            name="leave",
        )(role, x)
        held = jnp.asarray(TABLE)
        got = [shift(v, caps, helpers, d) for v, d in zip(sent, OUT)]
        stay, *back = pl.pallas_call(
            filter_kernel,
            out_shape=[all_of] + [one] * SEG,
            in_specs=[smem] + [vmem] * (SEG + 3),
            out_specs=[vmem] * (SEG + 1),
            scratch_shapes=[pltpu.VMEM(all_of.shape, jnp.float32)],
            compiler_params=small,
            name="filter_lines",
        )(role, lines, *got, kinds, held)
        stay = exchange(stay)
        home = {}
        for v, d in zip(back, BACK):
            home[d] = shift(v, helpers, relays if d in FAR else caps, -d)
        for d in FAR:
            home[d] = shift(home[d], relays, caps, 0)
        home = [home[d] for d in BACK]
        out = pl.pallas_call(
            finish_kernel,
            out_shape=jax.ShapeDtypeStruct(x.shape, x.dtype),
            in_specs=[smem, either] + [vmem] * (SEG + 1),
            out_specs=either,
            scratch_shapes=[
                pltpu.VMEM((SEG, PACK, rows), jnp.float32),
                pltpu.VMEM((2, SEG // 2, points, rows), jnp.float32),
                pltpu.SemaphoreType.DMA((2 * SEG + 2,)),
            ],
            input_output_aliases={1: 0},
            compiler_params=small,
            name="finish",
        )(role, base, stay, *home)
        return out.reshape(fields.shape)

    return jax.shard_map(
        on_device,
        mesh=mesh,
        in_specs=(P(None, "row", "phi", "theta"), P()),
        out_specs=P(None, "row", "phi", "theta"),
        check_vma=False,
    )
```

```python
import math

import jax
import jax.numpy as jnp
import numpy as np
from jax import lax
from jax.experimental import pallas as pl
from jax.experimental.pallas import tpu as pltpu
from jax.sharding import PartitionSpec as P

KMAX = 384
NPHI = 1536
SEG = 8
LOC = NPHI // SEG
MODES = KMAX // SEG
HALF = math.sqrt(0.5)


def cos_sin(k):
    turns = (k[:, None] * np.arange(LOC)[None, :]) % NPHI
    angle = turns * (2.0 * math.pi / NPHI)
    return np.cos(angle), np.sin(angle)


def matrices():
    m = SEG * np.arange(MODES)
    real = [np.concatenate(cos_sin(k)) for k in (m, m + 4)]
    paired = []
    for p in (1, 2, 3):
        cp, sp = cos_sin(m + p)
        cn, sn = cos_sin(m + SEG - p)
        paired.append(np.block([[cp, -sp], [cn, sn], [sp, cp], [sn, -cn]]))
    return real, paired


def parts(m):
    high = m.astype(jnp.bfloat16)
    return high, (m - high.astype(np.float64)).astype(jnp.bfloat16)


def table():
    real, paired = matrices()
    blocks, places, at = [], {}, 0

    def put(*columns):
        nonlocal at
        left = 0
        for key, m in columns:
            places.setdefault(key, []).append((at, m.shape[0], left, m.shape[1]))
            left += m.shape[1]
        blocks.append(np.concatenate([m for _, m in columns], axis=1))
        at += blocks[-1].shape[0]

    for i, m in enumerate(paired):
        for part in parts(m):
            put((("analysis", i + 2), part))
    back = [parts(m.T) for m in paired]
    for n in range(2):
        put((("synthesis", 2), back[0][n]), (("synthesis", 3), back[1][n]))
    put((("synthesis", 4), back[2][0]), (("synthesis", 4), back[2][1]))
    ahead = [parts(m) for m in real]
    for n in range(2):
        put((("analysis", 0), ahead[0][n]), (("analysis", 1), ahead[1][n]))
    put(*((("synthesis", i), part) for i in range(2) for part in parts(real[i].T)))
    return np.concatenate(blocks), places


TABLE, PLACES = table()
PACK = LOC // 2
SIZE = LOC + PACK
HOME = SEG + SEG // 2
FAR = (4, 3, 5, 2, 6)
OUT = (4, 3, 5, 2, 6, 1, 7, 0)
BACK = (4, 0, 3, 5, 1, 2, 7, 6)


def halves(x):
    high = x.astype(jnp.bfloat16)
    low = (x - high.astype(jnp.float32)).astype(jnp.bfloat16)
    return jnp.concatenate([high, low], axis=1)


def quarters(r):
    n, c = r.shape[0] // 2, r.shape[1] // 2
    return r[:n, :c] + (r[:n, c:] + r[n:, :c] + r[n:, c:])


def class_modes(*offsets):
    m = SEG * lax.broadcasted_iota(jnp.int32, (MODES, 128), 0)
    return jnp.concatenate([m + p for p in offsets], axis=0)


def filter_lines(y, counts, table_ref):
    def dot(key, i, x):
        rows = [table_ref[r : r + n, c : c + w] for r, n, c, w in PLACES[key, i]]
        rows = jnp.concatenate(rows, axis=0)
        return quarters(lax.dot_general(rows, x, (((1,), (0,)), ((), ())), preferred_element_type=jnp.float32))

    def keep(coef, k):
        weight = jnp.where(k == 0, 1.0 / NPHI, 2.0 / NPHI)
        return halves(jnp.where(k < counts, coef * weight, 0.0))

    e = [y[i] + y[i + 4] for i in range(4)]
    o = [y[i] - y[i + 4] for i in range(4)]
    e02, e13 = e[0] + e[2], e[1] + e[3]
    od, os_ = HALF * (o[1] - o[3]), HALF * (o[1] + o[3])
    pairs = [
        (o[0] + od, o[2] + os_),
        (e[0] - e[2], e[1] - e[3]),
        (o[0] - od, os_ - o[2]),
    ]
    u = []
    for i, x in enumerate((e02 + e13, e02 - e13)):
        coef = dot("analysis", i, halves(x))
        u.append(dot("synthesis", i, keep(coef, class_modes(4 * i, 4 * i))))
    su, du = u[0] + u[1], u[0] - u[1]
    uv = []
    for i, x in enumerate(pairs):
        coef = dot("analysis", i + 2, halves(jnp.concatenate(x, axis=0)))
        p = i + 1
        r = dot("synthesis", i + 2, keep(coef, class_modes(p, SEG - p, p, SEG - p)))
        uv.append((r[:LOC], r[LOC:]))
    (u1, v1), (u2, v2), (u3, v3) = uv
    p = [su + u2, du + v2, su - u2, du - v2]
    d13, s13 = HALF * (u1 - u3), HALF * (v1 + v3)
    q = [u1 + u3, s13 + d13, v1 - v3, s13 - d13]
    return [p[i] + q[i] for i in range(4)] + [p[i] - q[i] for i in range(4)]


def swap(v):
    return pltpu.roll(v, 64, 1)


def low_lanes():
    return lax.broadcasted_iota(jnp.int32, (PACK, 128), 1) < 64


def pack(v, half):
    top, bottom = v[:PACK], v[PACK:]
    if half:
        return jnp.where(low_lanes(), swap(top), bottom)
    return jnp.where(low_lanes(), top, swap(bottom))


def unpack(even, odd):
    return jnp.where(low_lanes(), even, swap(odd)), jnp.where(low_lanes(), swap(even), odd)


def place(role_ref, d):
    return lax.rem(role_ref[1] + SEG + role_ref[2] * d, SEG)


def run(copies):
    for c in copies:
        c.start()
    for c in copies:
        c.wait()


def stay_kernel(role_ref, x_ref, o_ref):
    @pl.when(role_ref[0] == 1)
    def _():
        for z in range(SEG):
            o_ref[z, :LOC] = x_ref[z]
            o_ref[z, LOC:] = pack(x_ref[SEG + z // 2], z % 2)


def leave_kernel(role_ref, x_ref, *refs):
    sent, (o_ref, packed, sem) = refs[:SEG], refs[SEG:]

    @pl.when(role_ref[0] == 1)
    def _():
        for z in range(SEG):
            packed[z] = pack(x_ref[HOME + SEG + z // 2], z % 2)
        for sent_ref, d in zip(sent, OUT):
            z = place(role_ref, d)
            sent_ref[:LOC] = x_ref[HOME + z]
            sent_ref[LOC:] = packed[z]

    @pl.when(role_ref[0] != 1)
    def _():
        run([pltpu.make_async_copy(x_ref, o_ref, sem)])


def filter_kernel(role_ref, lines_ref, *refs):
    got, (counts_ref, table_ref), refs = refs[:SEG], refs[SEG : SEG + 2], refs[SEG + 2 :]
    stay_ref, back, turned = refs[0], refs[1 : SEG + 1], refs[SEG + 1]

    def apply(source, target):
        done = filter_lines([source[s, :LOC] for s in range(SEG)], counts_ref[0:1], table_ref)
        for s in range(SEG):
            target[s, :LOC] = done[s]
        half = [source[s, LOC:] for s in range(SEG)]
        half = [jnp.concatenate([v, swap(v)], axis=0) for v in half]
        done = filter_lines(half, counts_ref[1:2], table_ref)
        for s in range(SEG):
            target[s, LOC:] = pack(done[s], 0)

    @pl.when(role_ref[0] == 1)
    def _():
        apply(lines_ref, stay_ref)

    @pl.when(role_ref[0] == 2)
    def _():
        for got_ref, d in zip(got, OUT):
            turned[place(role_ref, -d)] = got_ref[...]
        apply(turned, turned)
        for back_ref, d in zip(back, BACK):
            back_ref[...] = turned[place(role_ref, -d)]


def finish_kernel(role_ref, base_ref, stay_ref, *refs):
    home, (o_ref, packed, whole, sem) = refs[:SEG], refs[SEG:]
    del base_ref

    @pl.when(role_ref[0] == 1)
    def _():
        copies = []
        for z in range(SEG):
            copies.append(pltpu.make_async_copy(stay_ref.at[z, pl.ds(0, LOC)], o_ref.at[z], sem.at[z]))
        for d, home_ref in zip(BACK, home):
            z = place(role_ref, d)
            source = home_ref.at[pl.ds(0, LOC)]
            copies.append(pltpu.make_async_copy(source, o_ref.at[HOME + z], sem.at[SEG + d]))
        for c in copies:
            c.start()
        for d, home_ref in zip(BACK, home):
            packed[place(role_ref, d)] = home_ref[LOC:]
        for i in range(SEG // 2):
            for n, (even, odd) in enumerate(
                (
                    (stay_ref[2 * i, LOC:], stay_ref[2 * i + 1, LOC:]),
                    (packed[2 * i], packed[2 * i + 1]),
                )
            ):
                top, bottom = unpack(even, odd)
                whole[n, i, :PACK] = top
                whole[n, i, PACK:] = bottom
        last = []
        for n, first in enumerate((SEG, HOME + SEG)):
            target = o_ref.at[pl.ds(first, SEG // 2)]
            last.append(pltpu.make_async_copy(whole.at[n], target, sem.at[2 * SEG + n]))
        for c in last:
            c.start()
        for c in copies + last:
            c.wait()


def solution(mesh):
    n_phi, n_theta, n_row = (mesh.shape[a] for a in ("phi", "theta", "row"))
    last = n_theta - 1
    caps, helpers, relays = ((a, a + 1, last - 1 - a, last - a) for a in (0, 2, 4))

    def at(z, t, r):
        return (z * n_theta + t) * n_row + r

    groups = [[at(z, t, r) for z in range(n_phi)] for t in caps for r in range(n_row)]
    for t in range(2, last - 1, 2):
        for z in range(n_phi):
            groups.append([at(z, t + c, r) for r in range(n_row) for c in range(2)])

    def pairs(sources, targets, d):
        return [
            (z * n_theta + a, (z + (d if a % 2 == 0 else -d)) % n_phi * n_theta + b)
            for z in range(n_phi)
            for a, b in zip(sources, targets)
        ]

    def shift(v, sources, targets, d):
        return lax.ppermute(v, ("phi", "theta"), pairs(sources, targets, d))

    smem, vmem, either = (pl.BlockSpec(memory_space=m) for m in (pltpu.SMEM, pltpu.VMEM, pl.ANY))
    small = pltpu.CompilerParams(vmem_limit_bytes=16 << 20)

    def exchange(v):
        return lax.all_to_all(
            v,
            ("phi", "theta", "row"),
            split_axis=0,
            concat_axis=0,
            tiled=True,
            axis_index_groups=groups,
        )

    def on_device(fields, kept_counts):
        nf, shells, points, rows = fields.shape
        total = nf * shells
        theta, z = lax.axis_index("theta"), lax.axis_index("phi")
        is_cap = (theta < 2) | (theta > last - 2)
        is_helper = ((theta >= 2) & (theta < 4)) | ((theta > last - 4) & (theta <= last - 2))
        kind = jnp.where(is_cap, 1, jnp.where(is_helper, 2, 0))
        role = jnp.stack([kind, z, 1 - 2 * jnp.bitwise_and(theta, 1)]).astype(jnp.int32)
        band = jnp.bitwise_and(theta, 1) + jnp.where(theta < n_theta // 2, 0, 2)
        counts = lax.dynamic_slice(kept_counts, (band * rows,), (rows,)).reshape(1, rows)
        x = fields.reshape(total, points, rows)
        kinds = jnp.concatenate([counts, jnp.where(z % 2 == 0, counts, jnp.roll(counts, 64, axis=1))])
        one = jax.ShapeDtypeStruct((SIZE, rows), jnp.float32)
        all_of = jax.ShapeDtypeStruct((SEG, SIZE, rows), jnp.float32)
        kept = pl.pallas_call(
            stay_kernel,
            out_shape=all_of,
            in_specs=[smem, vmem],
            out_specs=vmem,
            compiler_params=small,
            name="stay",
        )(role, x)
        lines = exchange(kept)
        *sent, base = pl.pallas_call(
            leave_kernel,
            out_shape=[one] * SEG + [jax.ShapeDtypeStruct(x.shape, x.dtype)],
            in_specs=[smem, vmem],
            out_specs=[vmem] * SEG + [either],
            scratch_shapes=[pltpu.VMEM((SEG, PACK, rows), jnp.float32), pltpu.SemaphoreType.DMA],
            compiler_params=small,
            name="leave",
        )(role, x)
        held = jnp.asarray(TABLE)
        got = [shift(v, caps, helpers, d) for v, d in zip(sent, OUT)]
        stay, *back = pl.pallas_call(
            filter_kernel,
            out_shape=[all_of] + [one] * SEG,
            in_specs=[smem] + [vmem] * (SEG + 3),
            out_specs=[vmem] * (SEG + 1),
            scratch_shapes=[pltpu.VMEM(all_of.shape, jnp.float32)],
            compiler_params=small,
            name="filter_lines",
        )(role, lines, *got, kinds, held)
        stay = exchange(stay)
        home = {}
        for v, d in zip(back, BACK):
            home[d] = shift(v, helpers, relays if d in FAR else caps, -d)
        for d in FAR:
            home[d] = shift(home[d], relays, caps, 0)
        home = [home[d] for d in BACK]
        out = pl.pallas_call(
            finish_kernel,
            out_shape=jax.ShapeDtypeStruct(x.shape, x.dtype),
            in_specs=[smem, either] + [vmem] * (SEG + 1),
            out_specs=either,
            scratch_shapes=[
                pltpu.VMEM((SEG, PACK, rows), jnp.float32),
                pltpu.VMEM((2, SEG // 2, points, rows), jnp.float32),
                pltpu.SemaphoreType.DMA((2 * SEG + 2,)),
            ],
            input_output_aliases={1: 0},
            compiler_params=small,
            name="finish",
        )(role, base, stay, *home)
        return out.reshape(fields.shape)

    return jax.shard_map(
        on_device,
        mesh=mesh,
        in_specs=(P(None, "row", "phi", "theta"), P()),
        out_specs=P(None, "row", "phi", "theta"),
        check_vma=False,
    )
```

```python
import math

import jax
import jax.numpy as jnp
import numpy as np
from jax import lax
from jax.experimental import pallas as pl
from jax.experimental.pallas import tpu as pltpu
from jax.sharding import PartitionSpec as P

KMAX = 384
NPHI = 1536
SEG = 8
LOC = NPHI // SEG
MODES = KMAX // SEG
HALF = math.sqrt(0.5)


def cos_sin(k):
    turns = (k[:, None] * np.arange(LOC)[None, :]) % NPHI
    angle = turns * (2.0 * math.pi / NPHI)
    return np.cos(angle), np.sin(angle)


def matrices():
    m = SEG * np.arange(MODES)
    real = [np.concatenate(cos_sin(k)) for k in (m, m + 4)]
    paired = []
    for p in (1, 2, 3):
        cp, sp = cos_sin(m + p)
        cn, sn = cos_sin(m + SEG - p)
        paired.append(np.block([[cp, -sp], [cn, sn], [sp, cp], [sn, -cn]]))
    return paired, real + [a.T for a in paired], [a.T for a in real]


def stacked(group):
    parts = []
    for m in group:
        high = m.astype(jnp.bfloat16)
        parts += [high, (m - high.astype(np.float64)).astype(jnp.bfloat16)]
    return np.concatenate(parts)


TABLES = [stacked(g) for g in matrices()]
PLACES = [[2 * sum(m.shape[0] for m in g[:i]) for i in range(len(g) + 1)] for g in matrices()]
STAY = 2 * SEG
ORDER = (4, 3, 5, 2, 6, 1, 7, 0)


def halves(x):
    high = x.astype(jnp.bfloat16)
    low = (x - high.astype(jnp.float32)).astype(jnp.bfloat16)
    return jnp.concatenate([high, low], axis=1)


def quarters(r):
    n, c = r.shape[0] // 2, r.shape[1] // 2
    return r[:n, :c] + (r[:n, c:] + r[n:, :c] + r[n:, c:])


def class_modes(*offsets):
    m = SEG * lax.broadcasted_iota(jnp.int32, (MODES, 128), 0)
    return jnp.concatenate([m + p for p in offsets], axis=0)


def filter_lines(y, counts, tables):
    def dot(g, i, x):
        rows = tables[g][PLACES[g][i] : PLACES[g][i + 1], :]
        return quarters(lax.dot_general(rows, x, (((1,), (0,)), ((), ())), preferred_element_type=jnp.float32))

    def keep(coef, k):
        weight = jnp.where(k == 0, 1.0 / NPHI, 2.0 / NPHI)
        return halves(jnp.where(k < counts, coef * weight, 0.0))

    e = [y[i] + y[i + 4] for i in range(4)]
    o = [y[i] - y[i + 4] for i in range(4)]
    e02, e13 = e[0] + e[2], e[1] + e[3]
    od, os_ = HALF * (o[1] - o[3]), HALF * (o[1] + o[3])
    pairs = [
        (o[0] + od, o[2] + os_),
        (e[0] - e[2], e[1] - e[3]),
        (o[0] - od, os_ - o[2]),
    ]
    u = []
    for i, x in enumerate((e02 + e13, e02 - e13)):
        coef = dot(1, i, halves(x))
        u.append(dot(2, i, keep(coef, class_modes(4 * i, 4 * i))))
    su, du = u[0] + u[1], u[0] - u[1]
    uv = []
    for i, x in enumerate(pairs):
        coef = dot(0, i, halves(jnp.concatenate(x, axis=0)))
        p = i + 1
        r = dot(1, 2 + i, keep(coef, class_modes(p, SEG - p, p, SEG - p)))
        uv.append((r[:LOC], r[LOC:]))
    (u1, v1), (u2, v2), (u3, v3) = uv
    p = [su + u2, du + v2, su - u2, du - v2]
    d13, s13 = HALF * (u1 - u3), HALF * (v1 + v3)
    q = [u1 + u3, s13 + d13, v1 - v3, s13 - d13]
    return [p[i] + q[i] for i in range(4)] + [p[i] - q[i] for i in range(4)]


def run(copies):
    for c in copies:
        c.start()
    for c in copies:
        c.wait()


def gather_kernel(role_ref, x_ref, *refs):
    sent, (o_ref, sem) = refs[:SEG], refs[SEG:]

    @pl.when(role_ref[0] == 1)
    def _():
        for sent_ref, d in zip(sent, ORDER):
            sent_ref[...] = x_ref[STAY + lax.rem(role_ref[1] + d, SEG)]

    @pl.when(role_ref[0] != 1)
    def _():
        run([pltpu.make_async_copy(x_ref, o_ref, sem)])


def filter_kernel(role_ref, lines_ref, *refs):
    got, (counts_ref, *tables), refs = refs[:SEG], refs[SEG : SEG + 4], refs[SEG + 4 :]
    stay_ref, back, turned = refs[0], refs[1 : SEG + 1], refs[SEG + 1]
    counts = counts_ref[...]

    @pl.when(role_ref[0] == 1)
    def _():
        done = filter_lines([lines_ref[s] for s in range(SEG)], counts, tables)
        for s in range(SEG):
            stay_ref[s] = done[s]

    @pl.when((role_ref[0] == 2) & (pl.program_id(0) == 0))
    def _():
        for got_ref, d in zip(got, ORDER):
            turned[lax.rem(role_ref[1] + SEG - d, SEG)] = got_ref[...]
        done = filter_lines([turned[s] for s in range(SEG)], counts, tables)
        for s in range(SEG):
            turned[s] = done[s]
        for back_ref, d in zip(back, ORDER):
            back_ref[...] = turned[lax.rem(role_ref[1] + SEG - d, SEG)]


def home_kernel(role_ref, base_ref, *refs):
    home, o_ref, sem = refs[:SEG], refs[SEG], refs[SEG + 1]
    del base_ref

    @pl.when(role_ref[0] == 1)
    def _():
        run(
            [
                pltpu.make_async_copy(v, o_ref.at[STAY + lax.rem(role_ref[1] + d, SEG)], sem.at[d])
                for v, d in zip(home, ORDER)
            ]
        )


def finish_kernel(role_ref, base_ref, stay_ref, o_ref, sem):
    del base_ref

    @pl.when(role_ref[0] == 1)
    def _():
        run([pltpu.make_async_copy(stay_ref, o_ref.at[pl.ds(0, STAY)], sem)])


def solution(mesh):
    n_phi, n_theta, n_row = (mesh.shape[a] for a in ("phi", "theta", "row"))
    last = n_theta - 1
    caps, helpers, relays = ((a, a + 1, last - 1 - a, last - a) for a in (0, 2, 4))

    def at(z, t, r):
        return (z * n_theta + t) * n_row + r

    groups = [[at(z, t, r) for z in range(n_phi)] for t in caps for r in range(n_row)]
    for t in range(2, last - 1, 2):
        for z in range(n_phi):
            groups.append([at(z, t + c, r) for r in range(n_row) for c in range(2)])

    def pairs(sources, targets, d):
        return [
            (z * n_theta + a, (z + d) % n_phi * n_theta + b)
            for z in range(n_phi)
            for a, b in zip(sources, targets)
        ]

    def shift(v, sources, targets, d):
        return lax.ppermute(v, ("phi", "theta"), pairs(sources, targets, d))

    smem, vmem, either = (pl.BlockSpec(memory_space=m) for m in (pltpu.SMEM, pltpu.VMEM, pl.ANY))
    small = pltpu.CompilerParams(vmem_limit_bytes=16 << 20)

    def exchange(v):
        return lax.all_to_all(
            v,
            ("phi", "theta", "row"),
            split_axis=0,
            concat_axis=0,
            tiled=True,
            axis_index_groups=groups,
        )

    def on_device(fields, kept_counts):
        nf, shells, points, rows = fields.shape
        total = nf * shells
        theta, z = lax.axis_index("theta"), lax.axis_index("phi")
        is_cap = (theta < 2) | (theta > last - 2)
        is_helper = ((theta >= 2) & (theta < 4)) | ((theta > last - 4) & (theta <= last - 2))
        role = jnp.stack([jnp.where(is_cap, 1, jnp.where(is_helper, 2, 0)), z]).astype(jnp.int32)
        band = jnp.bitwise_and(theta, 1) + jnp.where(theta < n_theta // 2, 0, 2)
        counts = lax.dynamic_slice(kept_counts, (band * rows,), (rows,)).reshape(1, rows)
        x = fields.reshape(total, points, rows)
        one = jax.ShapeDtypeStruct((points, rows), jnp.float32)
        lines = exchange(x[:STAY])
        *sent, base = pl.pallas_call(
            gather_kernel,
            out_shape=[one] * SEG + [jax.ShapeDtypeStruct(x.shape, x.dtype)],
            in_specs=[smem, vmem],
            out_specs=[vmem] * SEG + [either],
            scratch_shapes=[pltpu.SemaphoreType.DMA],
            compiler_params=small,
            name="gather_groups",
        )(role, x)
        got = [shift(v, caps, helpers, d) for v, d in zip(sent, ORDER)]
        one_set = pl.BlockSpec((SEG, None, points, rows), lambda i: (0, i, 0, 0))
        stay, *back = pl.pallas_call(
            filter_kernel,
            out_shape=[jax.ShapeDtypeStruct((SEG, 2, points, rows), jnp.float32)] + [one] * SEG,
            grid=(2,),
            in_specs=[smem, one_set] + [vmem] * (SEG + 4),
            out_specs=[one_set] + [vmem] * SEG,
            scratch_shapes=[pltpu.VMEM((SEG, points, rows), jnp.float32)],
            compiler_params=small,
            name="filter_lines",
        )(role, lines.reshape(SEG, 2, points, rows), *got, counts, *[jnp.asarray(t) for t in TABLES])
        stay = exchange(stay.reshape(STAY, points, rows))
        relayed = [shift(v, helpers, relays if d else caps, -d) for v, d in zip(back, ORDER)]
        home = [shift(v, relays, caps, 0) if d else v for v, d in zip(relayed, ORDER)]
        whole = jax.ShapeDtypeStruct(x.shape, x.dtype)
        base = pl.pallas_call(
            home_kernel,
            out_shape=whole,
            in_specs=[smem, either] + [vmem] * SEG,
            out_specs=either,
            scratch_shapes=[pltpu.SemaphoreType.DMA((SEG,))],
            input_output_aliases={1: 0},
            compiler_params=small,
            name="home",
        )(role, base, *home)
        out = pl.pallas_call(
            finish_kernel,
            out_shape=whole,
            in_specs=[smem, either, vmem],
            out_specs=either,
            scratch_shapes=[pltpu.SemaphoreType.DMA],
            input_output_aliases={1: 0},
            compiler_params=small,
            name="finish",
        )(role, base, stay)
        return out.reshape(fields.shape)

    return jax.shard_map(
        on_device,
        mesh=mesh,
        in_specs=(P(None, "row", "phi", "theta"), P()),
        out_specs=P(None, "row", "phi", "theta"),
        check_vma=False,
    )
```

```python
import math

import jax
import jax.numpy as jnp
import numpy as np
from jax import lax
from jax.experimental import pallas as pl
from jax.experimental.pallas import tpu as pltpu
from jax.sharding import PartitionSpec as P

KMAX = 384
NPHI = 1536
SEG = 8
LOC = NPHI // SEG
MODES = KMAX // SEG
HALF = math.sqrt(0.5)


def cos_sin(k):
    turns = (k[:, None] * np.arange(LOC)[None, :]) % NPHI
    angle = turns * (2.0 * math.pi / NPHI)
    return np.cos(angle), np.sin(angle)


def matrices():
    m = SEG * np.arange(MODES)
    real = [np.concatenate(cos_sin(k)) for k in (m, m + 4)]
    paired = []
    for p in (1, 2, 3):
        cp, sp = cos_sin(m + p)
        cn, sn = cos_sin(m + SEG - p)
        paired.append(np.block([[cp, -sp], [cn, sn], [sp, cp], [sn, -cn]]))
    return paired, real + [a.T for a in paired], [a.T for a in real]


def stacked(group):
    parts = []
    for m in group:
        high = m.astype(jnp.bfloat16)
        parts += [high, (m - high.astype(np.float64)).astype(jnp.bfloat16)]
    return np.concatenate(parts)


TABLES = [stacked(g) for g in matrices()]
PLACES = [[2 * sum(m.shape[0] for m in g[:i]) for i in range(len(g) + 1)] for g in matrices()]
STAY = 2 * SEG
TAIL = 32
CUT = LOC - TAIL
ORDER = (4, 3, 5, 2, 6, 1, 7, 0)


def halves(x):
    high = x.astype(jnp.bfloat16)
    low = (x - high.astype(jnp.float32)).astype(jnp.bfloat16)
    return jnp.concatenate([high, low], axis=1)


def quarters(r):
    n, c = r.shape[0] // 2, r.shape[1] // 2
    return r[:n, :c] + (r[:n, c:] + r[n:, :c] + r[n:, c:])


def class_modes(*offsets):
    m = SEG * lax.broadcasted_iota(jnp.int32, (MODES, 128), 0)
    return jnp.concatenate([m + p for p in offsets], axis=0)


def filter_lines(y, counts, tables):
    def dot(g, i, x):
        rows = tables[g][PLACES[g][i] : PLACES[g][i + 1], :]
        return quarters(lax.dot_general(rows, x, (((1,), (0,)), ((), ())), preferred_element_type=jnp.float32))

    def keep(coef, k):
        weight = jnp.where(k == 0, 1.0 / NPHI, 2.0 / NPHI)
        return halves(jnp.where(k < counts, coef * weight, 0.0))

    e = [y[i] + y[i + 4] for i in range(4)]
    o = [y[i] - y[i + 4] for i in range(4)]
    e02, e13 = e[0] + e[2], e[1] + e[3]
    od, os_ = HALF * (o[1] - o[3]), HALF * (o[1] + o[3])
    pairs = [
        (o[0] + od, o[2] + os_),
        (e[0] - e[2], e[1] - e[3]),
        (o[0] - od, os_ - o[2]),
    ]
    u = []
    for i, x in enumerate((e02 + e13, e02 - e13)):
        coef = dot(1, i, halves(x))
        u.append(dot(2, i, keep(coef, class_modes(4 * i, 4 * i))))
    su, du = u[0] + u[1], u[0] - u[1]
    uv = []
    for i, x in enumerate(pairs):
        coef = dot(0, i, halves(jnp.concatenate(x, axis=0)))
        p = i + 1
        r = dot(1, 2 + i, keep(coef, class_modes(p, SEG - p, p, SEG - p)))
        uv.append((r[:LOC], r[LOC:]))
    (u1, v1), (u2, v2), (u3, v3) = uv
    p = [su + u2, du + v2, su - u2, du - v2]
    d13, s13 = HALF * (u1 - u3), HALF * (v1 + v3)
    q = [u1 + u3, s13 + d13, v1 - v3, s13 - d13]
    return [p[i] + q[i] for i in range(4)] + [p[i] - q[i] for i in range(4)]


def run(copies):
    for c in copies:
        c.start()
    for c in copies:
        c.wait()


def gather_kernel(role_ref, x_ref, *refs):
    sent, (o_ref, sem) = refs[:SEG], refs[SEG:]

    @pl.when(role_ref[0] == 1)
    def _():
        for sent_ref, d in zip(sent, ORDER):
            sent_ref[...] = x_ref[STAY + lax.rem(role_ref[1] + d, SEG)]

    @pl.when(role_ref[0] != 1)
    def _():
        run([pltpu.make_async_copy(x_ref, o_ref, sem)])


def filter_kernel(role_ref, lines_ref, *refs):
    got, (counts_ref, *tables), refs = refs[:SEG], refs[SEG : SEG + 4], refs[SEG + 4 :]
    stay_ref, back, tails = refs[0], refs[1 : SEG + 1], refs[SEG + 1 : 2 * SEG + 1]
    turned = refs[2 * SEG + 1]
    counts = counts_ref[...]

    @pl.when(role_ref[0] == 1)
    def _():
        done = filter_lines([lines_ref[s] for s in range(SEG)], counts, tables)
        for s in range(SEG):
            stay_ref[s] = done[s][:CUT]
            turned[s, CUT:] = done[s][CUT:]
        for tail_ref, d in zip(tails, ORDER):
            tail_ref[pl.program_id(0)] = turned[lax.rem(role_ref[1] + d, SEG), CUT:]

    @pl.when((role_ref[0] == 2) & (pl.program_id(0) == 0))
    def _():
        for got_ref, d in zip(got, ORDER):
            turned[lax.rem(role_ref[1] + SEG - d, SEG)] = got_ref[...]
        done = filter_lines([turned[s] for s in range(SEG)], counts, tables)
        for s in range(SEG):
            turned[s] = done[s]
        for back_ref, d in zip(back, ORDER):
            back_ref[...] = turned[lax.rem(role_ref[1] + SEG - d, SEG)]


def home_kernel(role_ref, base_ref, *refs):
    home, tails, o_ref, sem = refs[:SEG], refs[SEG : 2 * SEG], refs[2 * SEG], refs[2 * SEG + 1]
    del base_ref

    @pl.when(role_ref[0] == 1)
    def _():
        copies = []
        for v, d in zip(home, ORDER):
            target = o_ref.at[STAY + lax.rem(role_ref[1] + d, SEG)]
            copies.append(pltpu.make_async_copy(v, target, sem.at[d]))
        for v, d in zip(tails, ORDER):
            owner = lax.rem(role_ref[1] + SEG - d, SEG)
            target = o_ref.at[pl.ds(2 * owner, 2), pl.ds(CUT, TAIL)]
            copies.append(pltpu.make_async_copy(v, target, sem.at[SEG + d]))
        run(copies)


def finish_kernel(role_ref, base_ref, stay_ref, o_ref, sem):
    del base_ref

    @pl.when(role_ref[0] == 1)
    def _():
        run([pltpu.make_async_copy(stay_ref, o_ref.at[pl.ds(0, STAY), pl.ds(0, CUT)], sem)])


def solution(mesh):
    n_phi, n_theta, n_row = (mesh.shape[a] for a in ("phi", "theta", "row"))
    last = n_theta - 1
    caps, helpers, relays = ((a, a + 1, last - 1 - a, last - a) for a in (0, 2, 4))

    def at(z, t, r):
        return (z * n_theta + t) * n_row + r

    groups = [[at(z, t, r) for z in range(n_phi)] for t in caps for r in range(n_row)]
    for t in range(2, last - 1, 2):
        for z in range(n_phi):
            groups.append([at(z, t + c, r) for r in range(n_row) for c in range(2)])

    def pairs(sources, targets, d):
        return [
            (z * n_theta + a, (z + d) % n_phi * n_theta + b)
            for z in range(n_phi)
            for a, b in zip(sources, targets)
        ]

    def shift(v, sources, targets, d):
        return lax.ppermute(v, ("phi", "theta"), pairs(sources, targets, d))

    smem, vmem, either = (pl.BlockSpec(memory_space=m) for m in (pltpu.SMEM, pltpu.VMEM, pl.ANY))
    small = pltpu.CompilerParams(vmem_limit_bytes=16 << 20)

    def exchange(v):
        return lax.all_to_all(
            v,
            ("phi", "theta", "row"),
            split_axis=0,
            concat_axis=0,
            tiled=True,
            axis_index_groups=groups,
        )

    def on_device(fields, kept_counts):
        nf, shells, points, rows = fields.shape
        total = nf * shells
        theta, z = lax.axis_index("theta"), lax.axis_index("phi")
        is_cap = (theta < 2) | (theta > last - 2)
        is_helper = ((theta >= 2) & (theta < 4)) | ((theta > last - 4) & (theta <= last - 2))
        role = jnp.stack([jnp.where(is_cap, 1, jnp.where(is_helper, 2, 0)), z]).astype(jnp.int32)
        band = jnp.bitwise_and(theta, 1) + jnp.where(theta < n_theta // 2, 0, 2)
        counts = lax.dynamic_slice(kept_counts, (band * rows,), (rows,)).reshape(1, rows)
        x = fields.reshape(total, points, rows)
        one = jax.ShapeDtypeStruct((points, rows), jnp.float32)
        lines = exchange(x[:STAY])
        *sent, base = pl.pallas_call(
            gather_kernel,
            out_shape=[one] * SEG + [jax.ShapeDtypeStruct(x.shape, x.dtype)],
            in_specs=[smem, vmem],
            out_specs=[vmem] * SEG + [either],
            scratch_shapes=[pltpu.SemaphoreType.DMA],
            compiler_params=small,
            name="gather_groups",
        )(role, x)
        got = [shift(v, caps, helpers, d) for v, d in zip(sent, ORDER)]
        one_set, cut_set = (
            pl.BlockSpec((SEG, None, n, rows), lambda i: (0, i, 0, 0)) for n in (points, CUT)
        )
        tail = jax.ShapeDtypeStruct((2, TAIL, rows), jnp.float32)
        stay, *rest = pl.pallas_call(
            filter_kernel,
            out_shape=[jax.ShapeDtypeStruct((SEG, 2, CUT, rows), jnp.float32)] + [one] * SEG + [tail] * SEG,
            grid=(2,),
            in_specs=[smem, one_set] + [vmem] * (SEG + 4),
            out_specs=[cut_set] + [vmem] * (2 * SEG),
            scratch_shapes=[pltpu.VMEM((SEG, points, rows), jnp.float32)],
            compiler_params=small,
            name="filter_lines",
        )(role, lines.reshape(SEG, 2, points, rows), *got, counts, *[jnp.asarray(t) for t in TABLES])
        stay = exchange(stay.reshape(STAY, CUT, rows))
        back, tails = rest[:SEG], rest[SEG:]
        relayed = [shift(v, helpers, relays if d else caps, -d) for v, d in zip(back, ORDER)]
        home = [shift(v, relays, caps, 0) if d else v for v, d in zip(relayed, ORDER)]
        tails = [shift(v, caps, helpers, d) if d else v for v, d in zip(tails, ORDER)]
        tails = [shift(v, helpers, caps, 0) if d else v for v, d in zip(tails, ORDER)]
        whole = jax.ShapeDtypeStruct(x.shape, x.dtype)
        base = pl.pallas_call(
            home_kernel,
            out_shape=whole,
            in_specs=[smem, either] + [vmem] * (2 * SEG),
            out_specs=either,
            scratch_shapes=[pltpu.SemaphoreType.DMA((2 * SEG,))],
            input_output_aliases={1: 0},
            compiler_params=small,
            name="home",
        )(role, base, *home, *tails)
        out = pl.pallas_call(
            finish_kernel,
            out_shape=whole,
            in_specs=[smem, either, vmem],
            out_specs=either,
            scratch_shapes=[pltpu.SemaphoreType.DMA],
            input_output_aliases={1: 0},
            compiler_params=small,
            name="finish",
        )(role, base, stay)
        return out.reshape(fields.shape)

    return jax.shard_map(
        on_device,
        mesh=mesh,
        in_specs=(P(None, "row", "phi", "theta"), P()),
        out_specs=P(None, "row", "phi", "theta"),
        check_vma=False,
    )
```

```python
import math

import jax
import jax.numpy as jnp
import numpy as np
from jax import lax
from jax.experimental import pallas as pl
from jax.experimental.pallas import tpu as pltpu
from jax.sharding import PartitionSpec as P

KMAX = 384
NPHI = 1536
SEG = 8
LOC = NPHI // SEG
MODES = KMAX // SEG
HALF = math.sqrt(0.5)


def cos_sin(k):
    turns = (k[:, None] * np.arange(LOC)[None, :]) % NPHI
    angle = turns * (2.0 * math.pi / NPHI)
    return np.cos(angle), np.sin(angle)


def matrices():
    m = SEG * np.arange(MODES)
    real = [np.concatenate(cos_sin(k)) for k in (m, m + 4)]
    paired = []
    for p in (1, 2, 3):
        cp, sp = cos_sin(m + p)
        cn, sn = cos_sin(m + SEG - p)
        paired.append(np.block([[cp, -sp], [cn, sn], [sp, cp], [sn, -cn]]))
    return paired, [a.T for a in paired], [a.T for a in real], [np.concatenate(real, axis=1)]


def stacked(group):
    parts = []
    for m in group:
        high = m.astype(jnp.bfloat16)
        parts += [high, (m - high.astype(np.float64)).astype(jnp.bfloat16)]
    return np.concatenate(parts)


TABLES = [stacked(g) for g in matrices()]
PLACES = [[2 * sum(m.shape[0] for m in g[:i]) for i in range(len(g) + 1)] for g in matrices()]
STAY = 2 * SEG
ORDER = (4, 3, 5, 2, 6, 1, 7, 0)


def halves(x):
    high = x.astype(jnp.bfloat16)
    low = (x - high.astype(jnp.float32)).astype(jnp.bfloat16)
    return jnp.concatenate([high, low], axis=1)


def quarters(r):
    n, c = r.shape[0] // 2, r.shape[1] // 2
    return r[:n, :c] + (r[:n, c:] + r[n:, :c] + r[n:, c:])


def class_modes(*offsets):
    m = SEG * lax.broadcasted_iota(jnp.int32, (MODES, 128), 0)
    return jnp.concatenate([m + p for p in offsets], axis=0)


def filter_lines(y, counts, tables):
    def dot(g, i, x, rows=None):
        if rows is None:
            rows = tables[g][PLACES[g][i] : PLACES[g][i + 1], :]
        return quarters(lax.dot_general(rows, x, (((1,), (0,)), ((), ())), preferred_element_type=jnp.float32))

    def keep(coef, k):
        weight = jnp.where(k == 0, 1.0 / NPHI, 2.0 / NPHI)
        return halves(jnp.where(k < counts, coef * weight, 0.0))

    e = [y[i] + y[i + 4] for i in range(4)]
    o = [y[i] - y[i + 4] for i in range(4)]
    e02, e13 = e[0] + e[2], e[1] + e[3]
    od, os_ = HALF * (o[1] - o[3]), HALF * (o[1] + o[3])
    pairs = [
        (o[0] + od, o[2] + os_),
        (e[0] - e[2], e[1] - e[3]),
        (o[0] - od, os_ - o[2]),
    ]
    u = []
    for i, x in enumerate((e02 + e13, e02 - e13)):
        coef = dot(3, 0, halves(x), tables[3][:, LOC * i : LOC * (i + 1)])
        u.append(dot(2, i, keep(coef, class_modes(4 * i, 4 * i))))
    su, du = u[0] + u[1], u[0] - u[1]
    uv = []
    for i, x in enumerate(pairs):
        coef = dot(0, i, halves(jnp.concatenate(x, axis=0)))
        p = i + 1
        r = dot(1, i, keep(coef, class_modes(p, SEG - p, p, SEG - p)))
        uv.append((r[:LOC], r[LOC:]))
    (u1, v1), (u2, v2), (u3, v3) = uv
    p = [su + u2, du + v2, su - u2, du - v2]
    d13, s13 = HALF * (u1 - u3), HALF * (v1 + v3)
    q = [u1 + u3, s13 + d13, v1 - v3, s13 - d13]
    return [p[i] + q[i] for i in range(4)] + [p[i] - q[i] for i in range(4)]


def run(copies):
    for c in copies:
        c.start()
    for c in copies:
        c.wait()


def gather_kernel(role_ref, x_ref, *refs):
    sent, (o_ref, sem) = refs[:SEG], refs[SEG:]

    @pl.when(role_ref[0] == 1)
    def _():
        for sent_ref, d in zip(sent, ORDER):
            sent_ref[...] = x_ref[STAY + lax.rem(role_ref[1] + d, SEG)]

    @pl.when(role_ref[0] != 1)
    def _():
        run([pltpu.make_async_copy(x_ref, o_ref, sem)])


def filter_kernel(role_ref, lines_ref, *refs):
    got, (counts_ref, *tables), refs = refs[:SEG], refs[SEG : SEG + 5], refs[SEG + 5 :]
    stay_ref, back, turned = refs[0], refs[1 : SEG + 1], refs[SEG + 1]
    counts = counts_ref[...]

    @pl.when(role_ref[0] == 1)
    def _():
        done = filter_lines([lines_ref[s] for s in range(SEG)], counts, tables)
        for s in range(SEG):
            stay_ref[s] = done[s]

    @pl.when((role_ref[0] == 2) & (pl.program_id(0) == 0))
    def _():
        for got_ref, d in zip(got, ORDER):
            turned[lax.rem(role_ref[1] + SEG - d, SEG)] = got_ref[...]
        done = filter_lines([turned[s] for s in range(SEG)], counts, tables)
        for s in range(SEG):
            turned[s] = done[s]
        for back_ref, d in zip(back, ORDER):
            back_ref[...] = turned[lax.rem(role_ref[1] + SEG - d, SEG)]


def home_kernel(role_ref, base_ref, *refs):
    home, o_ref, sem = refs[:SEG], refs[SEG], refs[SEG + 1]
    del base_ref

    @pl.when(role_ref[0] == 1)
    def _():
        run(
            [
                pltpu.make_async_copy(v, o_ref.at[STAY + lax.rem(role_ref[1] + d, SEG)], sem.at[d])
                for v, d in zip(home, ORDER)
            ]
        )


def finish_kernel(role_ref, base_ref, stay_ref, o_ref, sem):
    del base_ref

    @pl.when(role_ref[0] == 1)
    def _():
        run([pltpu.make_async_copy(stay_ref, o_ref.at[pl.ds(0, STAY)], sem)])


def solution(mesh):
    n_phi, n_theta, n_row = (mesh.shape[a] for a in ("phi", "theta", "row"))
    last = n_theta - 1
    caps, helpers, relays = ((a, a + 1, last - 1 - a, last - a) for a in (0, 2, 4))

    def at(z, t, r):
        return (z * n_theta + t) * n_row + r

    groups = [[at(z, t, r) for z in range(n_phi)] for t in caps for r in range(n_row)]
    for t in range(2, last - 1, 2):
        for z in range(n_phi):
            groups.append([at(z, t + c, r) for r in range(n_row) for c in range(2)])

    def pairs(sources, targets, d):
        return [
            (z * n_theta + a, (z + d) % n_phi * n_theta + b)
            for z in range(n_phi)
            for a, b in zip(sources, targets)
        ]

    def shift(v, sources, targets, d):
        return lax.ppermute(v, ("phi", "theta"), pairs(sources, targets, d))

    smem, vmem, either = (pl.BlockSpec(memory_space=m) for m in (pltpu.SMEM, pltpu.VMEM, pl.ANY))
    small = pltpu.CompilerParams(vmem_limit_bytes=16 << 20)

    def exchange(v):
        return lax.all_to_all(
            v,
            ("phi", "theta", "row"),
            split_axis=0,
            concat_axis=0,
            tiled=True,
            axis_index_groups=groups,
        )

    def on_device(fields, kept_counts):
        nf, shells, points, rows = fields.shape
        total = nf * shells
        theta, z = lax.axis_index("theta"), lax.axis_index("phi")
        is_cap = (theta < 2) | (theta > last - 2)
        is_helper = ((theta >= 2) & (theta < 4)) | ((theta > last - 4) & (theta <= last - 2))
        role = jnp.stack([jnp.where(is_cap, 1, jnp.where(is_helper, 2, 0)), z]).astype(jnp.int32)
        band = jnp.bitwise_and(theta, 1) + jnp.where(theta < n_theta // 2, 0, 2)
        counts = lax.dynamic_slice(kept_counts, (band * rows,), (rows,)).reshape(1, rows)
        x = fields.reshape(total, points, rows)
        one = jax.ShapeDtypeStruct((points, rows), jnp.float32)
        lines = exchange(x[:STAY])
        *sent, base = pl.pallas_call(
            gather_kernel,
            out_shape=[one] * SEG + [jax.ShapeDtypeStruct(x.shape, x.dtype)],
            in_specs=[smem, vmem],
            out_specs=[vmem] * SEG + [either],
            scratch_shapes=[pltpu.SemaphoreType.DMA],
            compiler_params=small,
            name="gather_groups",
        )(role, x)
        got = [shift(v, caps, helpers, d) for v, d in zip(sent, ORDER)]
        one_set = pl.BlockSpec((SEG, None, points, rows), lambda i: (0, i, 0, 0))
        stay, *back = pl.pallas_call(
            filter_kernel,
            out_shape=[jax.ShapeDtypeStruct((SEG, 2, points, rows), jnp.float32)] + [one] * SEG,
            grid=(2,),
            in_specs=[smem, one_set] + [vmem] * (SEG + 5),
            out_specs=[one_set] + [vmem] * SEG,
            scratch_shapes=[pltpu.VMEM((SEG, points, rows), jnp.float32)],
            compiler_params=small,
            name="filter_lines",
        )(role, lines.reshape(SEG, 2, points, rows), *got, counts, *[jnp.asarray(t) for t in TABLES])
        stay = exchange(stay.reshape(STAY, points, rows))
        relayed = [shift(v, helpers, relays if d else caps, -d) for v, d in zip(back, ORDER)]
        home = [shift(v, relays, caps, 0) if d else v for v, d in zip(relayed, ORDER)]
        whole = jax.ShapeDtypeStruct(x.shape, x.dtype)
        base = pl.pallas_call(
            home_kernel,
            out_shape=whole,
            in_specs=[smem, either] + [vmem] * SEG,
            out_specs=either,
            scratch_shapes=[pltpu.SemaphoreType.DMA((SEG,))],
            input_output_aliases={1: 0},
            compiler_params=small,
            name="home",
        )(role, base, *home)
        out = pl.pallas_call(
            finish_kernel,
            out_shape=whole,
            in_specs=[smem, either, vmem],
            out_specs=either,
            scratch_shapes=[pltpu.SemaphoreType.DMA],
            input_output_aliases={1: 0},
            compiler_params=small,
            name="finish",
        )(role, base, stay)
        return out.reshape(fields.shape)

    return jax.shard_map(
        on_device,
        mesh=mesh,
        in_specs=(P(None, "row", "phi", "theta"), P()),
        out_specs=P(None, "row", "phi", "theta"),
        check_vma=False,
    )
```
